1024 devices in a mesh: energy: 64 (over y, z), space: 16 (over x, core).
Axes of the slice: x: 8, y: 8, z: 8, core: 2. Of those that a mesh axis runs over, the one named last changes fastest.
Arguments:
- iso_green: bfloat16 [64, 32, 2, 192, 192], P('energy', 'space'), as said below
- coupling: bfloat16 [32, 192, 192], P('space')
- screened: bfloat16 [64, 32, 2, 192, 192], P('energy', 'space'), as said below
Outputs:
- sigma: bfloat16 [64, 32, 2, 192, 192], P('energy', 'space')
Inputs may be any that keep to these rules, and one draw needn't show every extreme that they name: `iso_green`: every complex [192, 192] block (real and imaginary parts) equals its own transpose. `screened`: every complex [192, 192] block (real and imaginary parts) equals its own transpose.
All inputs are finite; a program needn't handle non-finite values.
Results may differ from the reference program's by a relative error of at most 0.023.
Values may be sent and summed in bfloat16 or wider, within the bound.
No kernel may reach another device: no remote copies, remote signals or barrier semaphores. Data moves between devices by JAX's collectives and lax.ppermute only.
A program may use at most 32 MiB of HBM per device.

```python
import math
import jax
import jax.numpy as jnp
from jax import lax

B = 192
NE = 64
NBLK = 32


def draw_iso_green(key, part):
    key_own = jax.random.fold_in(key, 11)
    key_off, key_mag, key_phase = jax.random.split(key_own, 3)
    random_part = jax.random.normal(key_off, (NE, NBLK, 2, B, B), jnp.float32)
    magnitude = jnp.exp(jax.random.uniform(key_mag, (NE, NBLK, B), jnp.float32, math.log(0.85), math.log(0.97)))
    offdiag = (random_part + jnp.swapaxes(random_part, -1, -2)) * (0.15 / math.sqrt(2.0 * B))
    phases = jax.random.uniform(key_phase, (NE, NBLK, B), jnp.float32, -math.pi, 0.0)
    diagonal = jnp.stack([magnitude * jnp.cos(phases), magnitude * jnp.sin(phases)], axis=2)
    identity = jnp.eye(B, dtype=jnp.float32)
    return (offdiag + diagonal[..., None] * identity).astype(jnp.bfloat16)


def draw_coupling(key, part):
    key_own = jax.random.fold_in(key, 23)
    random_part = jax.random.normal(key_own, (NBLK, B, B), jnp.float32)
    identity = jnp.eye(B, dtype=jnp.float32)
    return (identity + random_part * (0.2 / math.sqrt(B))).astype(jnp.bfloat16)


def draw_screened(key, part):
    key_own = jax.random.fold_in(key, 37)
    random_part = jax.random.normal(key_own, (NE, NBLK, 2, B, B), jnp.float32)
    symmetric = (random_part + jnp.swapaxes(random_part, -1, -2)) * (0.05 * math.sqrt(B) / math.sqrt(2.0))
    return symmetric.astype(jnp.bfloat16)


def setup_inputs(seed: int = 0) -> dict:
    key_of = jax.random.split(jax.random.key(seed), 4)
    iso_green = draw_iso_green(jax.random.fold_in(key_of[3], 71), 0)
    coupling = draw_coupling(jax.random.fold_in(key_of[3], 71), 0)
    screened = draw_screened(jax.random.fold_in(key_of[3], 71), 0)
    return dict(iso_green=iso_green, coupling=coupling, screened=screened)


def complex_product(operand, factor, pattern):
    op_re = operand[:, 0].astype(jnp.float32)
    op_im = operand[:, 1].astype(jnp.float32)
    fa_re = factor[:, 0].astype(jnp.float32)
    fa_im = factor[:, 1].astype(jnp.float32)
    highest = lax.Precision.HIGHEST
    product_re = jnp.einsum(pattern, op_re, fa_re, precision=highest) - jnp.einsum(pattern, op_im, fa_im, precision=highest)
    product_im = jnp.einsum(pattern, op_re, fa_im, precision=highest) + jnp.einsum(pattern, op_im, fa_re, precision=highest)
    return jnp.stack([product_re, product_im], axis=1)

def sandwich(carried, factor, source):
    middle = complex_product(carried, factor, 'ekl,eml->ekm').astype(jnp.bfloat16)
    return (source.astype(jnp.float32) + complex_product(factor, middle, 'ekl,elm->ekm')).astype(jnp.bfloat16)

def chain_step(carried, inputs):
    updated = sandwich(carried, inputs[0], inputs[1])
    return (updated, updated)

def convolve_block(operands):
    green_block, screen_block = operands
    green_c = lax.complex(green_block[:, 0].astype(jnp.float32), green_block[:, 1].astype(jnp.float32))
    screen_c = lax.complex(screen_block[:, 0].astype(jnp.float32), screen_block[:, 1].astype(jnp.float32))
    spectrum = jnp.fft.fft(green_c, axis=0) * jnp.fft.fft(screen_c, axis=0)
    convolved = jnp.fft.ifft(spectrum, axis=0) / math.sqrt(NE)
    return jnp.stack([-jnp.imag(convolved), jnp.real(convolved)], axis=1).astype(jnp.bfloat16)

def reference(iso_green, coupling, screened):
    green_blocks = jnp.moveaxis(iso_green, 1, 0)
    transfer_blocks = jnp.einsum('ebckl,blm->beckm', iso_green.astype(jnp.float32), coupling.astype(jnp.float32), precision=lax.Precision.HIGHEST).astype(jnp.bfloat16)
    starting = jnp.zeros((NE, 2, B, B), jnp.bfloat16)
    connected = lax.scan(chain_step, starting, (transfer_blocks, green_blocks))[1]
    screen_blocks = jnp.moveaxis(screened, 1, 0)
    sigma_blocks = lax.map(convolve_block, (connected, screen_blocks))
    return jnp.moveaxis(sigma_blocks, 0, 1)
```

```python
import math

import jax
import jax.numpy as jnp
import numpy as np
from jax import lax
from jax.experimental import pallas as pl
from jax.experimental.pallas import tpu as pltpu
from jax.sharding import PartitionSpec as P

F32 = jnp.float32
BF16 = jnp.bfloat16
TILE = 64

VM = pl.BlockSpec(memory_space=pltpu.VMEM)
SM = pl.BlockSpec(memory_space=pltpu.SMEM)


def dot_nn(a, b):
    return lax.dot_general(a, b, (((1,), (0,)), ((), ())), preferred_element_type=F32)


def dot_nt(a, b):
    return lax.dot_general(a, b, (((1,), (1,)), ((), ())), preferred_element_type=F32)


def complex_product(a, b, dot):
    a_re, a_im = a
    b_re, b_im = b
    return dot(a_re, b_re) - dot(a_im, b_im), dot(a_re, b_im) + dot(a_im, b_re)


def rounded(pair):
    return pair[0].astype(BF16), pair[1].astype(BF16)


def sandwich(carried, factor, source):
    middle = rounded(complex_product(carried, factor, dot_nt))
    re, im = complex_product(factor, middle, dot_nn)
    return rounded((source[0].astype(F32) + re, source[1].astype(F32) + im))


def pack(m):
    t = TILE
    return jnp.concatenate([m[:t, :], m[t : 2 * t, t:], m[2 * t :, 2 * t :]], axis=1)


def unpack(p):
    t = TILE
    p = p.astype(F32)
    t01, t02 = p[:, t : 2 * t], p[:, 2 * t : 3 * t]
    t11, t12 = p[:, 3 * t : 4 * t], p[:, 4 * t : 5 * t]
    top = p[:, : 3 * t]
    mid = jnp.concatenate([t01.T, t11, t12], axis=1)
    low = jnp.concatenate([t02.T, t12.T, p[:, 5 * t :]], axis=1)
    return jnp.concatenate([top, mid, low], axis=0).astype(BF16)


def load(ref, *at):
    return ref[(*at, 0)], ref[(*at, 1)]


def store(ref, pair, *at):
    ref[(*at, 0)] = pair[0]
    ref[(*at, 1)] = pair[1]


def local_kernel(green, coupling, screened, transfer, aggregate, packed):
    maps = []
    for b in range(2):
        k = coupling[b]
        g = load(green, b)
        t = rounded((dot_nn(g[0], k), dot_nn(g[1], k)))
        store(transfer, t, b)
        maps.append((t, g))
    (t0, g0), (t1, g1) = maps
    store(aggregate, rounded(complex_product(t1, t0, dot_nn)), 0)
    store(aggregate, sandwich(g0, t1, g1), 1)
    for b in range(2):
        for part in range(2):
            packed[2 * b + part] = pack(screened[b, part])


def compose_kernel(pairs, out):
    low = load(pairs, 0, 0), load(pairs, 0, 1)
    high = load(pairs, 1, 0), load(pairs, 1, 1)
    store(out, rounded(complex_product(high[0], low[0], dot_nn)), 0)
    store(out, sandwich(low[1], high[0], high[1]), 1)


def pair_kernel(pairs, out, end):
    low = load(pairs, 0, 0), load(pairs, 0, 1)
    high = load(pairs, 1, 0), load(pairs, 1, 1)
    store(out, rounded(complex_product(high[0], low[0], dot_nn)), 0)
    c = sandwich(low[1], high[0], high[1])
    store(out, c, 1)
    end[0] = pack(c[0])
    end[1] = pack(c[1])


def hop_kernel(hop, place, received, pair_map, end_in, prefix_in, end, prefix):
    mine = place[0] == hop

    @pl.when(mine)
    def _():
        before = unpack(received[0, 0]), unpack(received[0, 1])
        c = sandwich(before, load(pair_map, 0), load(pair_map, 1))
        end[0] = pack(c[0])
        end[1] = pack(c[1])
        prefix[...] = received[0]

    @pl.when(jnp.logical_not(mine))
    def _():
        end[...] = end_in[...]
        prefix[...] = prefix_in[...]


def final_kernel(hop, place, received, prefix_in, chips, cores, transfer, green, packed, state):
    mine = place[0] == hop

    @pl.when(mine)
    def _():
        state[0] = unpack(received[0, 0])
        state[1] = unpack(received[0, 1])

    @pl.when(jnp.logical_not(mine))
    def _():
        state[0] = unpack(prefix_in[0])
        state[1] = unpack(prefix_in[1])

    @pl.when(place[1] == 1)
    def _():
        store(state, sandwich(load(state), load(chips, 0, 0), load(chips, 0, 1)))

    @pl.when(place[2] == 1)
    def _():
        store(state, sandwich(load(state), load(cores, 0, 0), load(cores, 0, 1)))

    carried = load(state)
    for b in range(2):
        carried = sandwich(carried, load(transfer, b), load(green, b))
        packed[2 * b] = pack(carried[0])
        packed[2 * b + 1] = pack(carried[1])


def split(table):
    high = table.astype(jnp.bfloat16)
    return high, (table - high.astype(np.float32)).astype(jnp.bfloat16)


def tables(points):
    row = np.arange(points)
    angles = (row[:, None] * row[None, :] % points) * (2.0 * math.pi / points)
    cos, sin = np.cos(angles), np.sin(angles)
    forward = np.block([[cos, sin], [-sin, cos]]).astype(np.float32)
    scaling = 1.0 / (points * math.sqrt(points))
    inverse = (np.block([[-sin, -cos], [cos, -sin]]) * scaling).astype(np.float32)
    return np.concatenate(split(forward), axis=1), np.concatenate(split(inverse), axis=1)


def convolve_kernel(forward, inverse, values, out):
    half = values.shape[1] // 2
    width = half // 4
    x = values[...]
    re = jnp.concatenate([x[:, s : s + width] for s in range(0, 2 * half, 2 * width)], axis=1)
    im = jnp.concatenate([x[:, s : s + width] for s in range(width, 2 * half, 2 * width)], axis=1)
    joined = jnp.concatenate([re, im, re, im], axis=0)
    spectra = dot_nn(forward[...], joined)
    points = x.shape[0]
    g_re, g_im = spectra[:points, : 2 * width], spectra[points:, : 2 * width]
    s_re, s_im = spectra[:points, 2 * width :], spectra[points:, 2 * width :]
    product = jnp.concatenate([g_re * s_re - g_im * s_im, g_re * s_im + g_im * s_re], axis=0)
    high = product.astype(BF16)
    rest = (product - high.astype(F32)).astype(BF16)
    table = inverse[...]
    back = dot_nn(table, jnp.concatenate([high, high], axis=0)) + dot_nn(
        table[:, : 2 * points], rest
    )
    result = back.astype(BF16)
    for b in range(2):
        for part in range(2):
            out[:, (2 * b + part) * width : (2 * b + part + 1) * width] = result[
                part * points : (part + 1) * points, b * width : (b + 1) * width
            ]


def unpack_kernel(packed, out):
    for b in range(2):
        for part in range(2):
            out[b, part] = unpack(packed[2 * b + part])


def call(kernel, out_shapes, specs, scratch=(), interpret=False):
    many = isinstance(out_shapes, (list, tuple))
    return pl.pallas_call(
        kernel,
        out_shape=out_shapes,
        in_specs=specs,
        out_specs=[VM] * len(out_shapes) if many else VM,
        scratch_shapes=scratch,
        interpret=interpret,
    )


def shape(*dims):
    return jax.ShapeDtypeStruct(dims, BF16)


def chip_groups(pairs):
    return [[2 * low + core, 2 * high + core] for low, high in pairs for core in range(2)]


def scan_blocks(green, coupling, screened, interpret=False):
    n = green.shape[-1]
    width = 6 * TILE
    index = lax.axis_index("space")
    place = jnp.stack([index // 4, index // 2 % 2, index % 2]).astype(jnp.int32)
    transfer, aggregate, screen = call(
        local_kernel,
        [shape(2, 2, n, n), shape(2, 2, n, n), shape(4, TILE, width)],
        [VM] * 3,
        interpret=interpret,
    )(green, coupling, screened)

    def gather(x, groups):
        return lax.all_gather(x, "space", axis_index_groups=groups)

    cores = gather(aggregate, [[2 * c, 2 * c + 1] for c in range(8)])
    chip = call(compose_kernel, shape(2, 2, n, n), [VM], interpret=interpret)(cores)
    chips = gather(chip, chip_groups([(0, 1), (2, 3), (4, 5), (6, 7)]))
    pair_map, end = call(
        pair_kernel, [shape(2, 2, n, n), shape(2, TILE, width)], [VM], interpret=interpret
    )(chips)
    prefix = jnp.zeros_like(end)
    odd = chip_groups([(0, 2), (1, 3), (4, 6), (5, 7)])
    even = chip_groups([(2, 4), (3, 5), (6, 0), (7, 1)])
    for hop in (1, 2):
        received = gather(end, odd if hop % 2 else even)
        end, prefix = call(
            lambda *refs, hop=hop: hop_kernel(hop, *refs),
            [shape(2, TILE, width), shape(2, TILE, width)],
            [SM] + [VM] * 4,
            interpret=interpret,
        )(place, received, pair_map, end, prefix)
    received = gather(end, odd)
    connected = call(
        lambda *refs: final_kernel(3, *refs),
        shape(4, TILE, width),
        [SM] + [VM] * 6,
        scratch=[pltpu.VMEM((2, n, n), BF16)],
        interpret=interpret,
    )(place, received, prefix, chips, cores, transfer, green)
    return connected, screen


def shards(iso_green, coupling, screened):
    points = lax.axis_size("energy")
    n = iso_green.shape[-1]
    width = 6 * TILE
    connected, screen = scan_blocks(iso_green[0], coupling, screened[0])
    sent = jnp.concatenate([connected, screen], axis=0).transpose(1, 0, 2).reshape(points, -1)
    values = lax.all_to_all(sent, "energy", split_axis=0, concat_axis=0, tiled=True)
    forward, inverse = tables(points)
    result = call(convolve_kernel, shape(points, 4 * width), [VM] * 3)(
        jnp.asarray(forward), jnp.asarray(inverse), values
    )
    returned = lax.all_to_all(result, "energy", split_axis=0, concat_axis=0, tiled=True)
    packed = returned.reshape(points, 4, width).transpose(1, 0, 2)
    return call(unpack_kernel, shape(2, 2, n, n), [VM])(packed)[None]


def solution(mesh):
    in_specs = (
        P("energy", "space", None, None, None),
        P("space", None, None),
        P("energy", "space", None, None, None),
    )
    out_specs = P("energy", "space", None, None, None)
    return jax.shard_map(shards, mesh=mesh, in_specs=in_specs, out_specs=out_specs, check_vma=False)
```

```python
import math

import jax
import jax.numpy as jnp
import numpy as np
from jax import lax
from jax.experimental import pallas as pl
from jax.experimental.pallas import tpu as pltpu
from jax.sharding import PartitionSpec as P

F32 = jnp.float32
BF16 = jnp.bfloat16
TILE = 64
VMEM_GRANT = 16 * 2**20

VM = pl.BlockSpec(memory_space=pltpu.VMEM)


def dot_nn(a, b):
    return lax.dot_general(a, b, (((1,), (0,)), ((), ())), preferred_element_type=F32)


def dot_nt(a, b):
    return lax.dot_general(a, b, (((1,), (1,)), ((), ())), preferred_element_type=F32)


def complex_product(a, b, dot):
    a_re, a_im = a
    b_re, b_im = b
    return dot(a_re, b_re) - dot(a_im, b_im), dot(a_re, b_im) + dot(a_im, b_re)


def rounded(pair):
    return pair[0].astype(BF16), pair[1].astype(BF16)


def sandwich(carried, factor, source):
    middle = rounded(complex_product(carried, factor, dot_nt))
    re, im = complex_product(factor, middle, dot_nn)
    return rounded((source[0].astype(F32) + re, source[1].astype(F32) + im))


def pack(m):
    t = TILE
    return jnp.concatenate([m[:t, :], m[t : 2 * t, t:], m[2 * t :, 2 * t :]], axis=1)


def unpack(p):
    t = TILE
    p = p.astype(F32)
    t01, t02 = p[:, t : 2 * t], p[:, 2 * t : 3 * t]
    t11, t12 = p[:, 3 * t : 4 * t], p[:, 4 * t : 5 * t]
    top = p[:, : 3 * t]
    mid = jnp.concatenate([t01.T, t11, t12], axis=1)
    low = jnp.concatenate([t02.T, t12.T, p[:, 5 * t :]], axis=1)
    return jnp.concatenate([top, mid, low], axis=0).astype(BF16)


def load(ref, *at):
    return ref[(*at, 0)], ref[(*at, 1)]


def store(ref, pair, *at):
    ref[(*at, 0)] = pair[0]
    ref[(*at, 1)] = pair[1]


def local_kernel(green, coupling, transfer, aggregate):
    maps = []
    for b in range(2):
        k = coupling[b]
        g = load(green, b)
        t = rounded((dot_nn(g[0], k), dot_nn(g[1], k)))
        store(transfer, t, b)
        maps.append((t, g))
    (t0, g0), (t1, g1) = maps
    store(aggregate, rounded(complex_product(t1, t0, dot_nn)), 0)
    store(aggregate, sandwich(g0, t1, g1), 1)


def compose_kernel(pairs, out):
    low = load(pairs, 0, 0), load(pairs, 0, 1)
    high = load(pairs, 1, 0), load(pairs, 1, 1)
    store(out, rounded(complex_product(high[0], low[0], dot_nn)), 0)
    store(out, sandwich(low[1], high[0], high[1]), 1)


def pair_kernel(pairs, screened, out, end, prefix, screen):
    prefix[...] = jnp.zeros(prefix.shape, BF16)
    low = load(pairs, 0, 0), load(pairs, 0, 1)
    high = load(pairs, 1, 0), load(pairs, 1, 1)
    store(out, rounded(complex_product(high[0], low[0], dot_nn)), 0)
    c = sandwich(low[1], high[0], high[1])
    store(out, c, 1)
    end[0] = pack(c[0])
    end[1] = pack(c[1])
    for b in range(2):
        for part in range(2):
            screen[2 * b + part] = pack(screened[b, part])


def hop_kernel(hop, received, pair_map, end_in, prefix_in, end, prefix):
    index = lax.axis_index("space")
    mine = index // 4 == hop

    @pl.when(mine)
    def _():
        before = unpack(received[0, 0]), unpack(received[0, 1])
        c = sandwich(before, load(pair_map, 0), load(pair_map, 1))
        end[0] = pack(c[0])
        end[1] = pack(c[1])
        prefix[...] = received[0]

    @pl.when(jnp.logical_not(mine))
    def _():
        end[...] = end_in[...]
        prefix[...] = prefix_in[...]


def rows_first(parts):
    return jnp.swapaxes(jnp.stack([p.astype(F32) for p in parts], axis=0), 0, 1).astype(BF16)


def final_kernel(hop, received, prefix_in, chips, cores, transfer, green, screen, sent, state):
    index = lax.axis_index("space")
    mine = index // 4 == hop

    @pl.when(mine)
    def _():
        state[0] = unpack(received[0, 0])
        state[1] = unpack(received[0, 1])

    @pl.when(jnp.logical_not(mine))
    def _():
        state[0] = unpack(prefix_in[0])
        state[1] = unpack(prefix_in[1])

    @pl.when(index // 2 % 2 == 1)
    def _():
        store(state, sandwich(load(state), load(chips, 0, 0), load(chips, 0, 1)))

    @pl.when(index % 2 == 1)
    def _():
        store(state, sandwich(load(state), load(cores, 0, 0), load(cores, 0, 1)))

    carried = load(state)
    parts = []
    for b in range(2):
        carried = sandwich(carried, load(transfer, b), load(green, b))
        parts += [pack(carried[0]), pack(carried[1])]
    sent[...] = rows_first(parts + [screen[j] for j in range(4)])


def split(table):
    high = table.astype(jnp.bfloat16)
    return high, (table - high.astype(np.float32)).astype(jnp.bfloat16)


def tables(points):
    row = np.arange(points)
    angles = (row[:, None] * row[None, :] % points) * (2.0 * math.pi / points)
    cos, sin = np.cos(angles), np.sin(angles)
    forward = np.block([[cos, sin], [-sin, cos]]).astype(np.float32)
    scaling = 1.0 / (points * math.sqrt(points))
    inverse = (np.block([[-sin, -cos], [cos, -sin]]) * scaling).astype(np.float32)
    return np.concatenate(split(forward), axis=1), np.concatenate(split(inverse), axis=1)


def convolve_kernel(forward, inverse, values, out):
    points, _, width = values.shape
    x = jnp.swapaxes(values[...].astype(F32), 0, 1).astype(BF16)
    re = jnp.concatenate([x[j] for j in (0, 2, 4, 6)], axis=1)
    im = jnp.concatenate([x[j] for j in (1, 3, 5, 7)], axis=1)
    joined = jnp.concatenate([re, im, re, im], axis=0)
    spectra = dot_nn(forward[...], joined)
    g_re, g_im = spectra[:points, : 2 * width], spectra[points:, : 2 * width]
    s_re, s_im = spectra[:points, 2 * width :], spectra[points:, 2 * width :]
    product = jnp.concatenate([g_re * s_re - g_im * s_im, g_re * s_im + g_im * s_re], axis=0)
    high = product.astype(BF16)
    rest = (product - high.astype(F32)).astype(BF16)
    table = inverse[...]
    back = dot_nn(table, jnp.concatenate([high, high], axis=0)) + dot_nn(
        table[:, : 2 * points], rest
    )
    out[...] = rows_first(
        [
            back[part * points : (part + 1) * points, b * width : (b + 1) * width]
            for b in range(2)
            for part in range(2)
        ]
    )


def unpack_kernel(packed, out):
    parts = jnp.swapaxes(packed[...].astype(F32), 0, 1)
    for b in range(2):
        for part in range(2):
            out[b, part] = unpack(parts[2 * b + part])


def call(kernel, out_shapes, specs, scratch=(), interpret=False):
    many = isinstance(out_shapes, (list, tuple))
    return pl.pallas_call(
        kernel,
        out_shape=out_shapes,
        in_specs=specs,
        out_specs=[VM] * len(out_shapes) if many else VM,
        scratch_shapes=scratch,
        compiler_params=pltpu.CompilerParams(vmem_limit_bytes=VMEM_GRANT),
        interpret=interpret,
    )


def shape(*dims):
    return jax.ShapeDtypeStruct(dims, BF16)


def chip_groups(pairs):
    return [[2 * low + core, 2 * high + core] for low, high in pairs for core in range(2)]


def scan_blocks(green, coupling, screened, interpret=False):
    n = green.shape[-1]
    width = 6 * TILE
    transfer, aggregate = call(
        local_kernel, [shape(2, 2, n, n), shape(2, 2, n, n)], [VM] * 2, interpret=interpret
    )(green, coupling)

    def gather(x, groups):
        return lax.all_gather(x, "space", axis_index_groups=groups)

    cores = gather(aggregate, [[2 * c, 2 * c + 1] for c in range(8)])
    chip = call(compose_kernel, shape(2, 2, n, n), [VM], interpret=interpret)(cores)
    chips = gather(chip, chip_groups([(0, 1), (2, 3), (4, 5), (6, 7)]))
    pair_map, end, prefix, screen = call(
        pair_kernel,
        [shape(2, 2, n, n)] + [shape(2, TILE, width)] * 2 + [shape(4, TILE, width)],
        [VM] * 2,
        interpret=interpret,
    )(chips, screened)
    outer = chip_groups([(0, 2), (1, 3), (4, 6), (5, 7)])
    inner = chip_groups([(0, 1), (2, 4), (3, 5), (6, 7)])
    for hop in (1, 2):
        received = gather(end, outer if hop % 2 else inner)
        end, prefix = call(
            lambda *refs, hop=hop: hop_kernel(hop, *refs),
            [shape(2, TILE, width), shape(2, TILE, width)],
            [VM] * 4,
            interpret=interpret,
        )(received, pair_map, end, prefix)
    received = gather(end, outer)
    return call(
        lambda *refs: final_kernel(3, *refs),
        shape(TILE, 8, width),
        [VM] * 7,
        scratch=[pltpu.VMEM((2, n, n), BF16)],
        interpret=interpret,
    )(received, prefix, chips, cores, transfer, green, screen)


def shards(iso_green, coupling, screened):
    points = lax.axis_size("energy")
    n = iso_green.shape[-1]
    width = 6 * TILE
    sent = scan_blocks(iso_green[0], coupling, screened[0])
    values = lax.all_to_all(sent, "energy", split_axis=0, concat_axis=0, tiled=True)
    forward, inverse = tables(points)
    result = call(convolve_kernel, shape(points, 4, width), [VM] * 3)(
        jnp.asarray(forward), jnp.asarray(inverse), values
    )
    returned = lax.all_to_all(result, "energy", split_axis=0, concat_axis=0, tiled=True)
    return call(unpack_kernel, shape(2, 2, n, n), [VM])(returned)[None]


def solution(mesh):
    in_specs = (
        P("energy", "space", None, None, None),
        P("space", None, None),
        P("energy", "space", None, None, None),
    )
    out_specs = P("energy", "space", None, None, None)
    return jax.shard_map(shards, mesh=mesh, in_specs=in_specs, out_specs=out_specs, check_vma=False)
```

```python
import math

import jax
import jax.numpy as jnp
import numpy as np
from jax import lax
from jax.experimental import pallas as pl
from jax.experimental.pallas import tpu as pltpu
from jax.sharding import PartitionSpec as P

F32 = jnp.float32
BF16 = jnp.bfloat16
TILE = 64
PACKED = 5 * TILE
MAP = 14 * TILE
VMEM_GRANT = 16 * 2**20

VM = pl.BlockSpec(memory_space=pltpu.VMEM)
HB = pl.BlockSpec(memory_space=pltpu.HBM)


def dot_nn(a, b):
    return lax.dot_general(a, b, (((1,), (0,)), ((), ())), preferred_element_type=F32)


def dot_nt(a, b):
    return lax.dot_general(a, b, (((1,), (1,)), ((), ())), preferred_element_type=F32)


def complex_product(a, b, dot):
    a_re, a_im = a
    b_re, b_im = b
    return dot(a_re, b_re) - dot(a_im, b_im), dot(a_re, b_im) + dot(a_im, b_re)


def rounded(pair):
    return pair[0].astype(BF16), pair[1].astype(BF16)


def sandwich(carried, factor, source):
    middle = rounded(complex_product(carried, factor, dot_nt))
    re, im = complex_product(factor, middle, dot_nn)
    return rounded((source[0].astype(F32) + re, source[1].astype(F32) + im))


def half_turn(x):
    return pltpu.roll(x, TILE, 1)


def place_of(shape):
    row = lax.broadcasted_iota(jnp.int32, shape, 0)
    col = lax.broadcasted_iota(jnp.int32, shape, 1)
    return row, col


def widened(x):
    return jnp.concatenate([x, x], axis=1)


def pack(m):
    t = TILE
    m = m.astype(F32)
    row, col = place_of((t, 2 * t))
    top, mid = m[:t, : 2 * t], m[t : 2 * t, : 2 * t]
    right = [widened(m[k * t : (k + 1) * t, 2 * t :]) for k in range(3)]
    left = col < t
    d1 = jnp.where(col == row + t, mid, 0.0)
    diagonal = jnp.sum(d1, axis=1, keepdims=True)
    spare = jnp.where(col == 0, diagonal, jnp.where((row == 2) & (col == 1), diagonal[:1], 0.0))
    shared = jnp.where(col - t >= row, half_turn(top), mid)
    last = jnp.where(col >= row, right[2], spare)
    return jnp.where(left, right[0], top), jnp.where(left, right[1], shared), last


def unpack(first, second, y):
    t = TILE
    row, col = place_of((t, 2 * t))
    left = col < t
    first_t, second_t = first.T, second.T
    t02, t01, t12, x_t = first_t[:t], first_t[t:], second_t[:t], second_t[t:]
    diagonal = jnp.where(row[:, :1] == 0, y[2:3, 1:2], y[:, :1])
    d0 = jnp.where(col >= row, half_turn(second), widened(x_t))
    d1 = jnp.where(
        col - t < row, second, jnp.where(col - t > row, widened(x_t), diagonal)
    )
    d2 = jnp.where((col >= row)[:, :t], y[:, :t], y[:, :t].T)
    wide = [
        jnp.where(left, d0, first),
        jnp.where(left, widened(t01), d1),
        jnp.where(left, widened(t02), widened(t12)),
    ]
    narrow = [first[:, :t], second[:, :t], d2]
    return jnp.concatenate(
        [jnp.concatenate(wide, axis=0), jnp.concatenate(narrow, axis=0)], axis=1
    ).astype(BF16)


def pack_pair(pair):
    (a_re, b_re, c_re), (a_im, b_im, c_im) = pack(pair[0]), pack(pair[1])
    _, col = place_of(c_re.shape)
    last = jnp.where(col < TILE, c_re, half_turn(c_im))
    return jnp.concatenate([a_re, b_re, a_im, b_im, last], axis=1)


def unpack_pair(p):
    p = p.astype(F32)
    parts = [p[:, 2 * TILE * k : 2 * TILE * (k + 1)] for k in range(5)]
    return unpack(parts[0], parts[1], parts[4]), unpack(parts[2], parts[3], half_turn(parts[4]))


def store_map(ref, a, c):
    n, w = 3 * TILE, 2 * TILE
    ref[:n] = a[0][:, :w]
    ref[n : 2 * n] = a[1][:, :w]
    ref[2 * n : 3 * n] = jnp.concatenate([a[0][:, w:], a[1][:, w:]], axis=1)
    packed = pack_pair(c).astype(BF16)
    for k in range(5):
        ref[3 * n + k * TILE : 3 * n + (k + 1) * TILE] = packed[:, k * w : (k + 1) * w]


def load_map(ref):
    n, w = 3 * TILE, 2 * TILE
    rest = ref[2 * n : 3 * n]
    a = (
        jnp.concatenate([ref[:n], rest[:, :TILE]], axis=1),
        jnp.concatenate([ref[n : 2 * n], rest[:, TILE:]], axis=1),
    )
    packed = [ref[3 * n + k * TILE : 3 * n + (k + 1) * TILE] for k in range(5)]
    return a, unpack_pair(jnp.concatenate(packed, axis=1))


def load(ref, *at):
    return ref[(*at, 0)], ref[(*at, 1)]


def store(ref, pair, *at):
    ref[(*at, 0)] = pair[0]
    ref[(*at, 1)] = pair[1]


def local_kernel(green, coupling, transfer, aggregate, green_in, coupling_in, arrived):
    copies = [
        (
            pltpu.make_async_copy(coupling.at[b], coupling_in.at[b], arrived.at[b, 0]),
            pltpu.make_async_copy(green.at[b, 0], green_in.at[b, 0], arrived.at[b, 1]),
            pltpu.make_async_copy(green.at[b, 1], green_in.at[b, 1], arrived.at[b, 2]),
        )
        for b in range(2)
    ]
    for block in copies:
        for copy in block:
            copy.start()
    maps = []
    for b in range(2):
        for copy in copies[b]:
            copy.wait()
        k = coupling_in[b]
        g = load(green_in, b)
        t = rounded((dot_nn(g[0], k), dot_nn(g[1], k)))
        store(transfer, t, b)
        maps.append((t, g))
    (t0, g0), (t1, g1) = maps
    store_map(aggregate, rounded(complex_product(t1, t0, dot_nn)), sandwich(g0, t1, g1))


def joined(maps):
    (a_low, c_low), (a_high, c_high) = load_map(maps.at[0]), load_map(maps.at[1])
    return rounded(complex_product(a_high, a_low, dot_nn)), sandwich(c_low, a_high, c_high)


def compose_kernel(maps, out):
    store_map(out, *joined(maps))


def pair_kernel(maps, screened, out, end, prefix, screen):
    prefix[...] = jnp.zeros(prefix.shape, BF16)
    a, c = joined(maps)
    store(out, a, 0)
    store(out, c, 1)
    end[...] = pack_pair(c).astype(BF16)
    for b in range(2):
        screen[b] = pack_pair(load(screened, b)).astype(BF16)


def hop_kernel(hop, received, pair_map, end_in, prefix_in, end, prefix):
    mine = lax.axis_index("space") // 4 == hop

    @pl.when(mine)
    def _():
        before = unpack_pair(received[0])
        end[...] = pack_pair(sandwich(before, load(pair_map, 0), load(pair_map, 1))).astype(BF16)
        prefix[...] = received[0]

    @pl.when(jnp.logical_not(mine))
    def _():
        end[...] = end_in[...]
        prefix[...] = prefix_in[...]


def rows_first(parts):
    return jnp.swapaxes(jnp.stack([p.astype(F32) for p in parts], axis=0), 0, 1).astype(BF16)


def final_kernel(hop, received, prefix_in, chips, cores, transfer, green, screen, sent, state):
    index = lax.axis_index("space")
    mine = index // 4 == hop

    @pl.when(mine)
    def _():
        store(state, unpack_pair(received[0]))

    @pl.when(jnp.logical_not(mine))
    def _():
        store(state, unpack_pair(prefix_in[...]))

    @pl.when(index // 2 % 2 == 1)
    def _():
        store(state, sandwich(load(state), *load_map(chips.at[0])))

    @pl.when(index % 2 == 1)
    def _():
        store(state, sandwich(load(state), *load_map(cores.at[0])))

    carried = load(state)
    parts = []
    for b in range(2):
        carried = sandwich(carried, load(transfer, b), load(green, b))
        parts.append(pack_pair(carried))
    sent[...] = rows_first(parts + [screen[0], screen[1]])


def split(table):
    high = table.astype(jnp.bfloat16)
    return high, (table - high.astype(np.float32)).astype(jnp.bfloat16)


def tables(points):
    row = np.arange(points)
    angles = (row[:, None] * row[None, :] % points) * (2.0 * math.pi / points)
    cos, sin = np.cos(angles), np.sin(angles)
    forward = np.block([[cos, sin], [-sin, cos]]).astype(np.float32)
    scaling = 1.0 / (points * math.sqrt(points))
    inverse = (np.block([[-sin, -cos], [cos, -sin]]) * scaling).astype(np.float32)
    return np.concatenate(split(forward), axis=1), np.concatenate(split(inverse), axis=1)


def convolve_kernel(forward, inverse, values, out):
    points, _, lanes = values.shape
    part = 4 * TILE
    x = jnp.swapaxes(values[...].astype(F32), 0, 1)
    _, col = place_of((points, 2 * TILE))
    left = col < TILE

    def mixed(first, second):
        return jnp.where(left, first, half_turn(second)), jnp.where(left, half_turn(first), second)

    re, im = [], []
    for k in (0, 2):
        last_re, last_im = mixed(x[k, :, 2 * part :], x[k + 1, :, 2 * part :])
        re += [x[k, :, :part], x[k + 1, :, :part], last_re]
        im += [x[k, :, part : 2 * part], x[k + 1, :, part : 2 * part], last_im]
    re = jnp.concatenate(re, axis=1).astype(BF16)
    im = jnp.concatenate(im, axis=1).astype(BF16)
    spectra = dot_nn(forward[...], jnp.concatenate([re, im, re, im], axis=0))
    g_re, g_im = spectra[:points, :lanes], spectra[points:, :lanes]
    s_re, s_im = spectra[:points, lanes:], spectra[points:, lanes:]
    product = jnp.concatenate([g_re * s_re - g_im * s_im, g_re * s_im + g_im * s_re], axis=0)
    high = product.astype(BF16)
    rest = (product - high.astype(F32)).astype(BF16)
    table = inverse[...]
    back = dot_nn(table, jnp.concatenate([high, high], axis=0)) + dot_nn(
        table[:, : 2 * points], rest
    )
    b_re, b_im = back[:points], back[points:]
    last = mixed(b_re[:, 2 * part :], b_im[:, 2 * part :])
    out[...] = rows_first(
        [
            jnp.concatenate(
                [b_re[:, b * part : (b + 1) * part], b_im[:, b * part : (b + 1) * part], last[b]],
                axis=1,
            )
            for b in range(2)
        ]
    )


def unpack_kernel(packed, out, block, left):
    parts = jnp.swapaxes(packed[...].astype(F32), 0, 1)
    copies = []
    for b in range(2):
        store(block, unpack_pair(parts[b]), b)
        copies.append(pltpu.make_async_copy(block.at[b], out.at[b], left.at[b]))
        copies[b].start()
    for copy in copies:
        copy.wait()


def call(kernel, out_shapes, specs, scratch=(), interpret=False, out_spec=VM):
    many = isinstance(out_shapes, (list, tuple))
    return pl.pallas_call(
        kernel,
        out_shape=out_shapes,
        in_specs=specs,
        out_specs=[out_spec] * len(out_shapes) if many else out_spec,
        scratch_shapes=scratch,
        compiler_params=pltpu.CompilerParams(vmem_limit_bytes=VMEM_GRANT),
        interpret=interpret,
    )


def shape(*dims):
    return jax.ShapeDtypeStruct(dims, BF16)


def chip_groups(pairs):
    return [[2 * low + core, 2 * high + core] for low, high in pairs for core in range(2)]


def scan_blocks(green, coupling, screened, interpret=False):
    n = green.shape[-1]
    transfer, aggregate = call(
        local_kernel,
        [shape(2, 2, n, n), shape(MAP, 2 * TILE)],
        [HB] * 2,
        scratch=[
            pltpu.VMEM((2, 2, n, n), BF16),
            pltpu.VMEM((2, n, n), BF16),
            pltpu.SemaphoreType.DMA((2, 3)),
        ],
        interpret=interpret,
    )(green, coupling)

    def gather(x, groups):
        return lax.all_gather(x, "space", axis_index_groups=groups)

    cores = gather(aggregate, [[2 * c, 2 * c + 1] for c in range(8)])
    chip = call(compose_kernel, shape(MAP, 2 * TILE), [VM], interpret=interpret)(cores)
    chips = gather(chip, chip_groups([(0, 1), (2, 3), (4, 5), (6, 7)]))
    pair_map, end, prefix, screen = call(
        pair_kernel,
        [shape(2, 2, n, n)] + [shape(TILE, 2 * PACKED)] * 2 + [shape(2, TILE, 2 * PACKED)],
        [VM] * 2,
        interpret=interpret,
    )(chips, screened)
    outer = chip_groups([(0, 2), (1, 3), (4, 6), (5, 7)])
    inner = chip_groups([(0, 1), (2, 4), (3, 5), (6, 7)])
    for hop in (1, 2):
        received = gather(end, outer if hop % 2 else inner)
        end, prefix = call(
            lambda *refs, hop=hop: hop_kernel(hop, *refs),
            [shape(TILE, 2 * PACKED)] * 2,
            [VM] * 4,
            interpret=interpret,
        )(received, pair_map, end, prefix)
    received = gather(end, outer)
    return call(
        lambda *refs: final_kernel(3, *refs),
        shape(TILE, 4, 2 * PACKED),
        [VM] * 7,
        scratch=[pltpu.VMEM((2, n, n), BF16)],
        interpret=interpret,
    )(received, prefix, chips, cores, transfer, green, screen)


def shards(iso_green, coupling, screened):
    points = lax.axis_size("energy")
    n = iso_green.shape[-1]
    sent = scan_blocks(iso_green[0], coupling, screened[0])
    values = lax.all_to_all(sent, "energy", split_axis=0, concat_axis=0, tiled=True)
    forward, inverse = tables(points)
    result = call(convolve_kernel, shape(points, 2, 2 * PACKED), [VM] * 3)(
        jnp.asarray(forward), jnp.asarray(inverse), values
    )
    returned = lax.all_to_all(result, "energy", split_axis=0, concat_axis=0, tiled=True)
    return call(
        unpack_kernel,
        shape(2, 2, n, n),
        [VM],
        scratch=[pltpu.VMEM((2, 2, n, n), BF16), pltpu.SemaphoreType.DMA((2,))],
        out_spec=HB,
    )(returned)[None]


def solution(mesh):
    in_specs = (
        P("energy", "space", None, None, None),
        P("space", None, None),
        P("energy", "space", None, None, None),
    )
    out_specs = P("energy", "space", None, None, None)
    return jax.shard_map(shards, mesh=mesh, in_specs=in_specs, out_specs=out_specs, check_vma=False)
```

```python
import math

import jax
import jax.numpy as jnp
import numpy as np
from jax import lax
from jax.experimental import pallas as pl
from jax.experimental.pallas import tpu as pltpu
from jax.sharding import PartitionSpec as P

F32 = jnp.float32
BF16 = jnp.bfloat16
TILE = 64
PACKED = 5 * TILE
MAP = 14 * TILE
VMEM_GRANT = 16 * 2**20
FIRST_GRANT = 62 * 2**20

VM = pl.BlockSpec(memory_space=pltpu.VMEM)
HB = pl.BlockSpec(memory_space=pltpu.HBM)


def dot_nn(a, b):
    return lax.dot_general(a, b, (((1,), (0,)), ((), ())), preferred_element_type=F32)


def dot_nt(a, b):
    return lax.dot_general(a, b, (((1,), (1,)), ((), ())), preferred_element_type=F32)


def complex_product(a, b, dot):
    a_re, a_im = a
    b_re, b_im = b
    return dot(a_re, b_re) - dot(a_im, b_im), dot(a_re, b_im) + dot(a_im, b_re)


def rounded(pair):
    return pair[0].astype(BF16), pair[1].astype(BF16)


def sandwich(carried, factor, source):
    middle = rounded(complex_product(carried, factor, dot_nt))
    re, im = complex_product(factor, middle, dot_nn)
    return rounded((source[0].astype(F32) + re, source[1].astype(F32) + im))


def half_turn(x):
    return pltpu.roll(x, TILE, 1)


def place_of(shape):
    row = lax.broadcasted_iota(jnp.int32, shape, 0)
    col = lax.broadcasted_iota(jnp.int32, shape, 1)
    return row, col


def widened(x):
    return jnp.concatenate([x, x], axis=1)


def pack(m):
    t = TILE
    m = m.astype(F32)
    row, col = place_of((t, 2 * t))
    top, mid = m[:t, : 2 * t], m[t : 2 * t, : 2 * t]
    right = [widened(m[k * t : (k + 1) * t, 2 * t :]) for k in range(3)]
    left = col < t
    d1 = jnp.where(col == row + t, mid, 0.0)
    diagonal = jnp.sum(d1, axis=1, keepdims=True)
    spare = jnp.where(col == 0, diagonal, jnp.where((row == 2) & (col == 1), diagonal[:1], 0.0))
    shared = jnp.where(col - t >= row, half_turn(top), mid)
    last = jnp.where(col >= row, right[2], spare)
    return jnp.where(left, right[0], top), jnp.where(left, right[1], shared), last


def unpack(first, second, y):
    t = TILE
    row, col = place_of((t, 2 * t))
    left = col < t
    first_t, second_t = first.T, second.T
    t02, t01, t12, x_t = first_t[:t], first_t[t:], second_t[:t], second_t[t:]
    diagonal = jnp.where(row[:, :1] == 0, y[2:3, 1:2], y[:, :1])
    d0 = jnp.where(col >= row, half_turn(second), widened(x_t))
    d1 = jnp.where(
        col - t < row, second, jnp.where(col - t > row, widened(x_t), diagonal)
    )
    d2 = jnp.where((col >= row)[:, :t], y[:, :t], y[:, :t].T)
    wide = [
        jnp.where(left, d0, first),
        jnp.where(left, widened(t01), d1),
        jnp.where(left, widened(t02), widened(t12)),
    ]
    narrow = [first[:, :t], second[:, :t], d2]
    return jnp.concatenate(
        [jnp.concatenate(wide, axis=0), jnp.concatenate(narrow, axis=0)], axis=1
    ).astype(BF16)


def pack_pair(pair):
    (a_re, b_re, c_re), (a_im, b_im, c_im) = pack(pair[0]), pack(pair[1])
    _, col = place_of(c_re.shape)
    last = jnp.where(col < TILE, c_re, half_turn(c_im))
    return jnp.concatenate([a_re, b_re, a_im, b_im, last], axis=1)


def unpack_pair(p):
    p = p.astype(F32)
    parts = [p[:, 2 * TILE * k : 2 * TILE * (k + 1)] for k in range(5)]
    return unpack(parts[0], parts[1], parts[4]), unpack(parts[2], parts[3], half_turn(parts[4]))


def store_slabs(ref, start, packed):
    for k in range(5):
        ref[start + k * TILE : start + (k + 1) * TILE] = packed[:, 2 * k * TILE : 2 * (k + 1) * TILE]


def load_slabs(ref, start):
    slabs = [ref[start + k * TILE : start + (k + 1) * TILE] for k in range(5)]
    return jnp.concatenate(slabs, axis=1)


def store_map(ref, a, c):
    n, w = 3 * TILE, 2 * TILE
    ref[:n] = a[0][:, :w]
    ref[n : 2 * n] = a[1][:, :w]
    ref[2 * n : 3 * n] = jnp.concatenate([a[0][:, w:], a[1][:, w:]], axis=1)
    store_slabs(ref, 3 * n, pack_pair(c).astype(BF16))


def load_map(ref):
    n, w = 3 * TILE, 2 * TILE
    rest = ref[2 * n : 3 * n]
    a = (
        jnp.concatenate([ref[:n], rest[:, :TILE]], axis=1),
        jnp.concatenate([ref[n : 2 * n], rest[:, TILE:]], axis=1),
    )
    return a, unpack_pair(load_slabs(ref, 3 * n))


def load(ref, *at):
    return ref[(*at, 0)], ref[(*at, 1)]


def store(ref, pair, *at):
    ref[(*at, 0)] = pair[0]
    ref[(*at, 1)] = pair[1]


def local_kernel(
    green, coupling, screened, transfer, aggregate, green_in, coupling_in, screened_in, arrived
):
    copies = [
        [
            pltpu.make_async_copy(coupling.at[b], coupling_in.at[b], arrived.at[b, 0]),
            pltpu.make_async_copy(green.at[b, 0], green_in.at[b, 0], arrived.at[b, 1]),
            pltpu.make_async_copy(green.at[b, 1], green_in.at[b, 1], arrived.at[b, 2]),
        ]
        for b in range(2)
    ]
    later = [
        pltpu.make_async_copy(screened.at[b], screened_in.at[b], arrived.at[b, 3])
        for b in range(2)
    ]
    for copy in copies[0] + copies[1] + later:
        copy.start()
    maps = []
    for b in range(2):
        for copy in copies[b]:
            copy.wait()
        k = coupling_in[b]
        g = load(green_in, b)
        t = rounded((dot_nn(g[0], k), dot_nn(g[1], k)))
        store(transfer, t, b)
        maps.append((t, g))
    (t0, g0), (t1, g1) = maps
    store_map(aggregate, rounded(complex_product(t1, t0, dot_nn)), sandwich(g0, t1, g1))
    for b in range(2):
        later[b].wait()
        store_slabs(aggregate, MAP + b * PACKED, pack_pair(load(screened_in, b)).astype(BF16))


def joined(maps):
    (a_low, c_low), (a_high, c_high) = load_map(maps.at[0]), load_map(maps.at[1])
    return rounded(complex_product(a_high, a_low, dot_nn)), sandwich(c_low, a_high, c_high)


def compose_kernel(maps, out):
    store_map(out, *joined(maps))


def pair_kernel(maps, out, end, prefix):
    prefix[...] = jnp.zeros(prefix.shape, BF16)
    a, c = joined(maps)
    store(out, a, 0)
    store(out, c, 1)
    end[...] = pack_pair(c).astype(BF16)


def hop_kernel(hop, received, pair_map, end_in, prefix_in, end, prefix):
    mine = lax.axis_index("space") // 4 == hop

    @pl.when(mine)
    def _():
        before = unpack_pair(received[0])
        end[...] = pack_pair(sandwich(before, load(pair_map, 0), load(pair_map, 1))).astype(BF16)
        prefix[...] = received[0]

    @pl.when(jnp.logical_not(mine))
    def _():
        end[...] = end_in[...]
        prefix[...] = prefix_in[...]


def rows_first(parts):
    return jnp.swapaxes(jnp.stack([p.astype(F32) for p in parts], axis=0), 0, 1).astype(BF16)


def entry_kernel(hop, received, prefix, chips, entry, unused):
    index = lax.axis_index("space")
    mine = index // 4 == hop
    before = jnp.where(mine, received[0], prefix[...])
    odd = index // 2 % 2 == 1
    unused[...] = jnp.zeros(unused.shape, BF16)
    entry[TILE:] = jnp.zeros((TILE, 2 * PACKED), BF16)

    @pl.when(odd)
    def _():
        c = sandwich(unpack_pair(before), *load_map(chips.at[0]))
        entry[:TILE] = pack_pair(c).astype(BF16)

    @pl.when(jnp.logical_not(odd))
    def _():
        entry[:TILE] = before


def screen_kernel(cores, sent):
    sent[...] = rows_first(
        [load_slabs(cores.at[core], MAP + b * PACKED) for core in range(2) for b in range(2)]
    )


def regroup_kernel(values, theirs, mine):
    x = jnp.swapaxes(values[...].astype(F32), 0, 1).astype(BF16)
    points = values.shape[0]
    for b in range(2):
        mine[b] = x[b]
        theirs[b * points : (b + 1) * points] = x[2 + b]


def final_kernel(shared, cores, transfer, green, sent, state):
    store(state, unpack_pair(shared[1, :TILE]))

    @pl.when(lax.axis_index("space") % 2 == 1)
    def _():
        store(state, sandwich(load(state), *load_map(cores.at[0])))

    carried = load(state)
    parts = []
    for b in range(2):
        carried = sandwich(carried, load(transfer, b), load(green, b))
        parts.append(pack_pair(carried))
    sent[...] = rows_first(parts)


def split(table):
    high = table.astype(jnp.bfloat16)
    return high, (table - high.astype(np.float32)).astype(jnp.bfloat16)


def tables(points):
    row = np.arange(points)
    angles = (row[:, None] * row[None, :] % points) * (2.0 * math.pi / points)
    cos, sin = np.cos(angles), np.sin(angles)
    forward = np.block([[cos, sin], [-sin, cos]]).astype(np.float32)
    scaling = 1.0 / (points * math.sqrt(points))
    inverse = (np.block([[-sin, -cos], [cos, -sin]]) * scaling).astype(np.float32)
    return np.concatenate(split(forward), axis=1), np.concatenate(split(inverse), axis=1)


def convolve_kernel(forward, inverse, values, shared, mine, out, screen):
    points, _, lanes = values.shape
    part = 4 * TILE
    even = lax.axis_index("space") % 2 == 0

    @pl.when(even)
    def _():
        screen[...] = mine[...]

    @pl.when(jnp.logical_not(even))
    def _():
        for b in range(2):
            screen[b] = shared[0, b * points : (b + 1) * points]

    g = jnp.swapaxes(values[...].astype(F32), 0, 1)
    x = [g[0], g[1], screen[0].astype(F32), screen[1].astype(F32)]
    _, col = place_of((points, 2 * TILE))
    left = col < TILE

    def mixed(first, second):
        return jnp.where(left, first, half_turn(second)), jnp.where(left, half_turn(first), second)

    re, im = [], []
    for k in (0, 2):
        last_re, last_im = mixed(x[k][:, 2 * part :], x[k + 1][:, 2 * part :])
        re += [x[k][:, :part], x[k + 1][:, :part], last_re]
        im += [x[k][:, part : 2 * part], x[k + 1][:, part : 2 * part], last_im]
    re = jnp.concatenate(re, axis=1).astype(BF16)
    im = jnp.concatenate(im, axis=1).astype(BF16)
    spectra = dot_nn(forward[...], jnp.concatenate([re, im, re, im], axis=0))
    g_re, g_im = spectra[:points, :lanes], spectra[points:, :lanes]
    s_re, s_im = spectra[:points, lanes:], spectra[points:, lanes:]
    product = jnp.concatenate([g_re * s_re - g_im * s_im, g_re * s_im + g_im * s_re], axis=0)
    high = product.astype(BF16)
    rest = (product - high.astype(F32)).astype(BF16)
    table = inverse[...]
    back = dot_nn(table, jnp.concatenate([high, high], axis=0)) + dot_nn(
        table[:, : 2 * points], rest
    )
    b_re, b_im = back[:points], back[points:]
    last = mixed(b_re[:, 2 * part :], b_im[:, 2 * part :])
    out[...] = rows_first(
        [
            jnp.concatenate(
                [b_re[:, b * part : (b + 1) * part], b_im[:, b * part : (b + 1) * part], last[b]],
                axis=1,
            )
            for b in range(2)
        ]
    )


def unpack_kernel(packed, out, block, left):
    parts = jnp.swapaxes(packed[...].astype(F32), 0, 1)
    copies = []
    for b in range(2):
        store(block, unpack_pair(parts[b]), b)
        copies.append(pltpu.make_async_copy(block.at[b], out.at[b], left.at[b]))
        copies[b].start()
    for copy in copies:
        copy.wait()


def call(kernel, out_shapes, specs, scratch=(), interpret=False, out_spec=VM, grant=VMEM_GRANT):
    many = isinstance(out_shapes, (list, tuple))
    return pl.pallas_call(
        kernel,
        out_shape=out_shapes,
        in_specs=specs,
        out_specs=[out_spec] * len(out_shapes) if many else out_spec,
        scratch_shapes=scratch,
        compiler_params=pltpu.CompilerParams(vmem_limit_bytes=grant),
        interpret=interpret,
    )


def shape(*dims):
    return jax.ShapeDtypeStruct(dims, BF16)


def chip_groups(pairs):
    return [[2 * low + core, 2 * high + core] for low, high in pairs for core in range(2)]


def scan_blocks(green, coupling, screened, exchange, interpret=False):
    n = green.shape[-1]
    transfer, aggregate = call(
        local_kernel,
        [shape(2, 2, n, n), shape(MAP + 2 * PACKED, 2 * TILE)],
        [HB] * 3,
        scratch=[
            pltpu.VMEM((2, 2, n, n), BF16),
            pltpu.VMEM((2, n, n), BF16),
            pltpu.VMEM((2, 2, n, n), BF16),
            pltpu.SemaphoreType.DMA((2, 4)),
        ],
        interpret=interpret,
        grant=FIRST_GRANT,
    )(green, coupling, screened)

    def gather(x, groups):
        return lax.all_gather(x, "space", axis_index_groups=groups)

    both = [[2 * c, 2 * c + 1] for c in range(8)]
    outer = chip_groups([(0, 2), (1, 3), (4, 6), (5, 7)])
    inner = chip_groups([(0, 1), (2, 4), (3, 5), (6, 7)])
    packed = shape(TILE, 2 * PACKED)
    points = TILE
    leaving = [shape(2 * points, 2 * PACKED), shape(2, points, 2 * PACKED)]

    def chain(cores):
        chip = call(compose_kernel, shape(MAP, 2 * TILE), [VM], interpret=interpret)(cores)
        chips = gather(chip, chip_groups([(0, 1), (2, 3), (4, 5), (6, 7)]))
        pair_map, end, prefix = call(
            pair_kernel, [shape(2, 2, n, n), packed, packed], [VM], interpret=interpret
        )(chips)
        for hop in (1, 2):
            received = gather(end, outer if hop % 2 else inner)
            end, prefix = call(
                lambda *refs, hop=hop: hop_kernel(hop, *refs),
                [packed] * 2,
                [VM] * 4,
                interpret=interpret,
            )(received, pair_map, end, prefix)
        received = gather(end, outer)
        return tuple(
            call(lambda *refs: entry_kernel(3, *refs), leaving, [VM] * 3, interpret=interpret)(
                received, prefix, chips
            )
        )

    def exchange_screen(cores):
        sent = call(screen_kernel, shape(TILE, 4, 2 * PACKED), [VM], interpret=interpret)(cores)
        return tuple(call(regroup_kernel, leaving, [VM], interpret=interpret)(exchange(sent)))

    cores = gather(aggregate, both)
    leave, mine = lax.cond(lax.axis_index("space") % 2 == 1, chain, exchange_screen, cores)
    shared = gather(leave, both)
    sent = call(
        final_kernel,
        shape(TILE, 2, 2 * PACKED),
        [VM] * 4,
        scratch=[pltpu.VMEM((2, n, n), BF16)],
        interpret=interpret,
    )(shared, cores, transfer, green)
    return sent, shared, mine


def shards(iso_green, coupling, screened):
    points = lax.axis_size("energy")
    n = iso_green.shape[-1]

    def exchange(x):
        return lax.all_to_all(x, "energy", split_axis=0, concat_axis=0, tiled=True)

    sent, shared, mine = scan_blocks(iso_green[0], coupling, screened[0], exchange)
    forward, inverse = tables(points)
    result = call(
        convolve_kernel,
        shape(points, 2, 2 * PACKED),
        [VM] * 5,
        scratch=[pltpu.VMEM((2, points, 2 * PACKED), BF16)],
    )(jnp.asarray(forward), jnp.asarray(inverse), exchange(sent), shared, mine)
    return call(
        unpack_kernel,
        shape(2, 2, n, n),
        [VM],
        scratch=[pltpu.VMEM((2, 2, n, n), BF16), pltpu.SemaphoreType.DMA((2,))],
        out_spec=HB,
    )(exchange(result))[None]


def solution(mesh):
    in_specs = (
        P("energy", "space", None, None, None),
        P("space", None, None),
        P("energy", "space", None, None, None),
    )
    out_specs = P("energy", "space", None, None, None)
    return jax.shard_map(shards, mesh=mesh, in_specs=in_specs, out_specs=out_specs, check_vma=False)
```

```python
import math

import jax
import jax.numpy as jnp
import numpy as np
from jax import lax
from jax.experimental import pallas as pl
from jax.experimental.pallas import tpu as pltpu
from jax.sharding import PartitionSpec as P

F32 = jnp.float32
BF16 = jnp.bfloat16
TILE = 64
PACKED = 5 * TILE
MAP = 14 * TILE
VMEM_GRANT = 16 * 2**20

VM = pl.BlockSpec(memory_space=pltpu.VMEM)
HB = pl.BlockSpec(memory_space=pltpu.HBM)


def dot_nn(a, b):
    return lax.dot_general(a, b, (((1,), (0,)), ((), ())), preferred_element_type=F32)


def dot_nt(a, b):
    return lax.dot_general(a, b, (((1,), (1,)), ((), ())), preferred_element_type=F32)


def complex_product(a, b, dot):
    a_re, a_im = a
    b_re, b_im = b
    return dot(a_re, b_re) - dot(a_im, b_im), dot(a_re, b_im) + dot(a_im, b_re)


def rounded(pair):
    return pair[0].astype(BF16), pair[1].astype(BF16)


def sandwich(carried, factor, source):
    middle = rounded(complex_product(carried, factor, dot_nt))
    re, im = complex_product(factor, middle, dot_nn)
    return rounded((source[0].astype(F32) + re, source[1].astype(F32) + im))


def half_turn(x):
    return pltpu.roll(x, TILE, 1)


def place_of(shape):
    row = lax.broadcasted_iota(jnp.int32, shape, 0)
    col = lax.broadcasted_iota(jnp.int32, shape, 1)
    return row, col


def widened(x):
    return jnp.concatenate([x, x], axis=1)


def sandwich_packed(carried, factor, source):
    middle = rounded(complex_product(carried, factor, dot_nt))
    total = pack_pair(complex_product(factor, middle, dot_nn)) + source.astype(F32)
    return total.astype(BF16)


def pack(m):
    t = TILE
    m = m.astype(F32)
    row, col = place_of((t, 2 * t))
    top, mid = m[:t, : 2 * t], m[t : 2 * t, : 2 * t]
    right = [widened(m[k * t : (k + 1) * t, 2 * t :]) for k in range(3)]
    left = col < t
    d1 = jnp.where(col == row + t, mid, 0.0)
    diagonal = jnp.sum(d1, axis=1, keepdims=True)
    spare = jnp.where(col == 0, diagonal, jnp.where((row == 2) & (col == 1), diagonal[:1], 0.0))
    shared = jnp.where(col - t >= row, half_turn(top), mid)
    last = jnp.where(col >= row, right[2], spare)
    return jnp.where(left, right[0], top), jnp.where(left, right[1], shared), last


def unpack(first, second, y):
    t = TILE
    row, col = place_of((t, 2 * t))
    left = col < t
    first_t, second_t = first.T, second.T
    t02, t01, t12, x_t = first_t[:t], first_t[t:], second_t[:t], second_t[t:]
    diagonal = jnp.where(row[:, :1] == 0, y[2:3, 1:2], y[:, :1])
    d0 = jnp.where(col >= row, half_turn(second), widened(x_t))
    d1 = jnp.where(
        col - t < row, second, jnp.where(col - t > row, widened(x_t), diagonal)
    )
    d2 = jnp.where((col >= row)[:, :t], y[:, :t], y[:, :t].T)
    wide = [
        jnp.where(left, d0, first),
        jnp.where(left, widened(t01), d1),
        jnp.where(left, widened(t02), widened(t12)),
    ]
    narrow = [first[:, :t], second[:, :t], d2]
    return jnp.concatenate(
        [jnp.concatenate(wide, axis=0), jnp.concatenate(narrow, axis=0)], axis=1
    ).astype(BF16)


def pack_pair(pair):
    (a_re, b_re, c_re), (a_im, b_im, c_im) = pack(pair[0]), pack(pair[1])
    _, col = place_of(c_re.shape)
    last = jnp.where(col < TILE, c_re, half_turn(c_im))
    return jnp.concatenate([a_re, b_re, a_im, b_im, last], axis=1)


def unpack_pair(p):
    p = p.astype(F32)
    parts = [p[:, 2 * TILE * k : 2 * TILE * (k + 1)] for k in range(5)]
    return unpack(parts[0], parts[1], parts[4]), unpack(parts[2], parts[3], half_turn(parts[4]))


def store_slabs(ref, start, packed):
    for k in range(5):
        ref[start + k * TILE : start + (k + 1) * TILE] = packed[:, 2 * k * TILE : 2 * (k + 1) * TILE]


def load_slabs(ref, start):
    slabs = [ref[start + k * TILE : start + (k + 1) * TILE] for k in range(5)]
    return jnp.concatenate(slabs, axis=1)


def store_map(ref, a, packed):
    n, w = 3 * TILE, 2 * TILE
    ref[:n] = a[0][:, :w]
    ref[n : 2 * n] = a[1][:, :w]
    ref[2 * n : 3 * n] = jnp.concatenate([a[0][:, w:], a[1][:, w:]], axis=1)
    store_slabs(ref, 3 * n, packed)


def load_map(ref):
    n, w = 3 * TILE, 2 * TILE
    rest = ref[2 * n : 3 * n]
    a = (
        jnp.concatenate([ref[:n], rest[:, :TILE]], axis=1),
        jnp.concatenate([ref[n : 2 * n], rest[:, TILE:]], axis=1),
    )
    return a, load_slabs(ref, 3 * n)


def load(ref, *at):
    return ref[(*at, 0)], ref[(*at, 1)]


def store(ref, pair, *at):
    ref[(*at, 0)] = pair[0]
    ref[(*at, 1)] = pair[1]


def local_kernel(
    green, coupling, screened, transfer, aggregate, green_in, coupling_in, screened_in, arrived
):
    copies = [
        [
            pltpu.make_async_copy(coupling.at[b], coupling_in.at[b], arrived.at[b, 0]),
            pltpu.make_async_copy(green.at[b, 0], green_in.at[b, 0], arrived.at[b, 1]),
            pltpu.make_async_copy(green.at[b, 1], green_in.at[b, 1], arrived.at[b, 2]),
        ]
        for b in range(2)
    ]
    later = [
        pltpu.make_async_copy(screened.at[b], screened_in.at[b], arrived.at[b, 3])
        for b in range(2)
    ]
    for copy in copies[0] + copies[1] + later:
        copy.start()
    maps = []
    for b in range(2):
        for copy in copies[b]:
            copy.wait()
        k = coupling_in[b]
        g = load(green_in, b)
        t = rounded((dot_nn(g[0], k), dot_nn(g[1], k)))
        if b == 0:
            store(transfer, t)
        maps.append((t, g))
    (t0, g0), (t1, g1) = maps
    c = pack_pair(sandwich(g0, t1, g1)).astype(BF16)
    store_map(aggregate, rounded(complex_product(t1, t0, dot_nn)), c)
    for b in range(2):
        later[b].wait()
        store_slabs(aggregate, MAP + b * PACKED, pack_pair(load(screened_in, b)).astype(BF16))


def joined(maps):
    (a_low, c_low), (a_high, c_high) = load_map(maps.at[0]), load_map(maps.at[1])
    a = rounded(complex_product(a_high, a_low, dot_nn))
    return a, sandwich_packed(unpack_pair(c_low), a_high, c_high)


def compose_kernel(maps, out):
    store_map(out, *joined(maps))


def pair_kernel(maps, out, end, prefix):
    prefix[...] = jnp.zeros(prefix.shape, BF16)
    a, c = joined(maps)
    store(out, a)
    end[...] = c


def hop_kernel(hop, received, pair_a, pair_c, end_in, prefix_in, end, prefix):
    mine = lax.axis_index("space") // 4 == hop

    @pl.when(mine)
    def _():
        before = received[0]
        end[...] = sandwich_packed(unpack_pair(before), load(pair_a), pair_c[...])
        prefix[...] = before

    @pl.when(jnp.logical_not(mine))
    def _():
        end[...] = end_in[...]
        prefix[...] = prefix_in[...]


def rows_first(parts):
    return jnp.swapaxes(jnp.stack([p.astype(F32) for p in parts], axis=0), 0, 1).astype(BF16)


def entry_kernel(hop, received, prefix, chips, entry, unused):
    index = lax.axis_index("space")
    mine = index // 4 == hop
    before = jnp.where(mine, received[0], prefix[...])
    odd = index // 2 % 2 == 1
    unused[...] = jnp.zeros(unused.shape, BF16)
    entry[TILE:] = jnp.zeros((TILE, 2 * PACKED), BF16)

    @pl.when(odd)
    def _():
        entry[:TILE] = sandwich_packed(unpack_pair(before), *load_map(chips.at[0]))

    @pl.when(jnp.logical_not(odd))
    def _():
        entry[:TILE] = before


def screen_kernel(cores, sent, last_map):
    last_map[...] = cores[0, :MAP]
    sent[...] = rows_first(
        [load_slabs(cores.at[core], MAP + b * PACKED) for core in range(2) for b in range(2)]
    )


def regroup_kernel(values, theirs, mine):
    x = jnp.swapaxes(values[...].astype(F32), 0, 1).astype(BF16)
    points = values.shape[0]
    for b in range(2):
        mine[b] = x[b]
        theirs[b * points : (b + 1) * points] = x[2 + b]


def final_kernel(shared, cores, last_map, transfer, green, sent, state):
    entry = unpack_pair(shared[1, :TILE])
    store(state, entry)

    @pl.when(lax.axis_index("space") % 2 == 1)
    def _():
        a, c = load_map(cores.at[0])
        store(state, sandwich(entry, a, unpack_pair(c)))

    last = sandwich_packed(entry, *load_map(last_map))
    first = sandwich(load(state), load(transfer), load(green, 0))
    sent[...] = rows_first([pack_pair(first), last])


def split(table):
    high = table.astype(jnp.bfloat16)
    return high, (table - high.astype(np.float32)).astype(jnp.bfloat16)


def tables(points):
    row = np.arange(points)
    angles = (row[:, None] * row[None, :] % points) * (2.0 * math.pi / points)
    cos, sin = np.cos(angles), np.sin(angles)
    forward = np.block([[cos, sin], [-sin, cos]]).astype(np.float32)
    scaling = 1.0 / (points * math.sqrt(points))
    inverse = (np.block([[-sin, -cos], [cos, -sin]]) * scaling).astype(np.float32)
    return np.concatenate(split(forward), axis=1), np.concatenate(split(inverse), axis=1)


def convolve_kernel(forward, inverse, values, shared, mine, out, screen):
    points, _, lanes = values.shape
    part = 4 * TILE
    even = lax.axis_index("space") % 2 == 0

    @pl.when(even)
    def _():
        screen[...] = mine[...]

    @pl.when(jnp.logical_not(even))
    def _():
        for b in range(2):
            screen[b] = shared[0, b * points : (b + 1) * points]

    g = jnp.swapaxes(values[...].astype(F32), 0, 1)
    x = [g[0], g[1], screen[0].astype(F32), screen[1].astype(F32)]
    _, col = place_of((points, 2 * TILE))
    left = col < TILE

    def mixed(first, second):
        return jnp.where(left, first, half_turn(second)), jnp.where(left, half_turn(first), second)

    re, im = [], []
    for k in (0, 2):
        last_re, last_im = mixed(x[k][:, 2 * part :], x[k + 1][:, 2 * part :])
        re += [x[k][:, :part], x[k + 1][:, :part], last_re]
        im += [x[k][:, part : 2 * part], x[k + 1][:, part : 2 * part], last_im]
    re = jnp.concatenate(re, axis=1).astype(BF16)
    im = jnp.concatenate(im, axis=1).astype(BF16)
    spectra = dot_nn(forward[...], jnp.concatenate([re, im, re, im], axis=0))
    g_re, g_im = spectra[:points, :lanes], spectra[points:, :lanes]
    s_re, s_im = spectra[:points, lanes:], spectra[points:, lanes:]
    product = jnp.concatenate([g_re * s_re - g_im * s_im, g_re * s_im + g_im * s_re], axis=0)
    high = product.astype(BF16)
    rest = (product - high.astype(F32)).astype(BF16)
    table = inverse[...]
    back = dot_nn(table, jnp.concatenate([high, high], axis=0)) + dot_nn(
        table[:, : 2 * points], rest
    )
    b_re, b_im = back[:points], back[points:]
    last = mixed(b_re[:, 2 * part :], b_im[:, 2 * part :])
    out[...] = rows_first(
        [
            jnp.concatenate(
                [b_re[:, b * part : (b + 1) * part], b_im[:, b * part : (b + 1) * part], last[b]],
                axis=1,
            )
            for b in range(2)
        ]
    )


def unpack_kernel(packed, out, block, left):
    parts = jnp.swapaxes(packed[...].astype(F32), 0, 1)
    copies = []
    for b in range(2):
        store(block, unpack_pair(parts[b]), b)
        copies.append(pltpu.make_async_copy(block.at[b], out.at[b], left.at[b]))
        copies[b].start()
    for copy in copies:
        copy.wait()


def call(kernel, out_shapes, specs, scratch=(), interpret=False, out_spec=VM):
    many = isinstance(out_shapes, (list, tuple))
    return pl.pallas_call(
        kernel,
        out_shape=out_shapes,
        in_specs=specs,
        out_specs=[out_spec] * len(out_shapes) if many else out_spec,
        scratch_shapes=scratch,
        compiler_params=pltpu.CompilerParams(vmem_limit_bytes=VMEM_GRANT),
        interpret=interpret,
    )


def shape(*dims):
    return jax.ShapeDtypeStruct(dims, BF16)


def chip_groups(pairs):
    return [[2 * low + core, 2 * high + core] for low, high in pairs for core in range(2)]


def scan_blocks(green, coupling, screened, exchange, interpret=False):
    n = green.shape[-1]
    transfer, aggregate = call(
        local_kernel,
        [shape(2, n, n), shape(MAP + 2 * PACKED, 2 * TILE)],
        [HB] * 3,
        scratch=[
            pltpu.VMEM((2, 2, n, n), BF16),
            pltpu.VMEM((2, n, n), BF16),
            pltpu.VMEM((2, 2, n, n), BF16),
            pltpu.SemaphoreType.DMA((2, 4)),
        ],
        interpret=interpret,
    )(*(pltpu.with_memory_space_constraint(x, pltpu.HBM) for x in (green, coupling, screened)))

    def gather(x, groups):
        return lax.all_gather(x, "space", axis_index_groups=groups)

    both = [[2 * c, 2 * c + 1] for c in range(8)]
    outer = chip_groups([(0, 2), (1, 3), (4, 6), (5, 7)])
    inner = chip_groups([(0, 1), (2, 4), (3, 5), (6, 7)])
    packed = shape(TILE, 2 * PACKED)
    points = TILE
    leaving = [shape(2 * points, 2 * PACKED), shape(2, points, 2 * PACKED)]

    def chain(cores):
        chip = call(compose_kernel, shape(MAP, 2 * TILE), [VM], interpret=interpret)(cores)
        chips = gather(chip, chip_groups([(0, 1), (2, 3), (4, 5), (6, 7)]))
        pair_a, end, prefix = call(
            pair_kernel, [shape(2, n, n), packed, packed], [VM], interpret=interpret
        )(chips)
        pair_c = end
        for hop in (1, 2):
            received = gather(end, outer if hop % 2 else inner)
            end, prefix = call(
                lambda *refs, hop=hop: hop_kernel(hop, *refs),
                [packed] * 2,
                [VM] * 5,
                interpret=interpret,
            )(received, pair_a, pair_c, end, prefix)
        received = gather(end, outer)
        leave, unused = call(
            lambda *refs: entry_kernel(3, *refs), leaving, [VM] * 3, interpret=interpret
        )(received, prefix, chips)
        return leave, unused, chip

    def exchange_screen(cores):
        sent, last_map = call(
            screen_kernel,
            [shape(TILE, 4, 2 * PACKED), shape(MAP, 2 * TILE)],
            [VM],
            interpret=interpret,
        )(cores)
        leave, mine = call(regroup_kernel, leaving, [VM], interpret=interpret)(exchange(sent))
        return leave, mine, last_map

    cores = gather(aggregate, both)
    odd = lax.axis_index("space") % 2 == 1
    leave, mine, last_map = lax.cond(odd, chain, exchange_screen, cores)
    shared = gather(leave, both)
    sent = call(
        final_kernel,
        shape(TILE, 2, 2 * PACKED),
        [VM] * 5,
        scratch=[pltpu.VMEM((2, n, n), BF16)],
        interpret=interpret,
    )(shared, cores, last_map, transfer, green)
    return sent, shared, mine


def shards(iso_green, coupling, screened):
    points = lax.axis_size("energy")
    n = iso_green.shape[-1]

    def exchange(x):
        return lax.all_to_all(x, "energy", split_axis=0, concat_axis=0, tiled=True)

    sent, shared, mine = scan_blocks(iso_green[0], coupling, screened[0], exchange)
    forward, inverse = tables(points)
    result = call(
        convolve_kernel,
        shape(points, 2, 2 * PACKED),
        [VM] * 5,
        scratch=[pltpu.VMEM((2, points, 2 * PACKED), BF16)],
    )(jnp.asarray(forward), jnp.asarray(inverse), exchange(sent), shared, mine)
    return call(
        unpack_kernel,
        shape(2, 2, n, n),
        [VM],
        scratch=[pltpu.VMEM((2, 2, n, n), BF16), pltpu.SemaphoreType.DMA((2,))],
        out_spec=HB,
    )(exchange(result))[None]


def solution(mesh):
    in_specs = (
        P("energy", "space", None, None, None),
        P("space", None, None),
        P("energy", "space", None, None, None),
    )
    out_specs = P("energy", "space", None, None, None)
    return jax.shard_map(shards, mesh=mesh, in_specs=in_specs, out_specs=out_specs, check_vma=False)
```

```python
import math

import jax
import jax.numpy as jnp
import numpy as np
from jax import lax
from jax.experimental import pallas as pl
from jax.experimental.pallas import tpu as pltpu
from jax.sharding import PartitionSpec as P

F32 = jnp.float32
BF16 = jnp.bfloat16
TILE = 64
PACKED = 5 * TILE
MAP = 14 * TILE
VMEM_GRANT = 16 * 2**20

VM = pl.BlockSpec(memory_space=pltpu.VMEM)
HB = pl.BlockSpec(memory_space=pltpu.HBM)


def dot_nn(a, b):
    return lax.dot_general(a, b, (((1,), (0,)), ((), ())), preferred_element_type=F32)


def dot_nt(a, b):
    return lax.dot_general(a, b, (((1,), (1,)), ((), ())), preferred_element_type=F32)


def complex_product(a, b, dot):
    a_re, a_im = a
    b_re, b_im = b
    return dot(a_re, b_re) - dot(a_im, b_im), dot(a_re, b_im) + dot(a_im, b_re)


def rounded(pair):
    return pair[0].astype(BF16), pair[1].astype(BF16)


def sandwich(carried, factor, source):
    middle = rounded(complex_product(carried, factor, dot_nt))
    re, im = complex_product(factor, middle, dot_nn)
    return rounded((source[0].astype(F32) + re, source[1].astype(F32) + im))


def half_turn(x):
    return pltpu.roll(x, TILE, 1)


def place_of(shape):
    row = lax.broadcasted_iota(jnp.int32, shape, 0)
    col = lax.broadcasted_iota(jnp.int32, shape, 1)
    return row, col


def widened(x):
    return jnp.concatenate([x, x], axis=1)


def sandwich_packed(carried, factor, source):
    middle = rounded(complex_product(carried, factor, dot_nt))
    total = pack_pair(complex_product(factor, middle, dot_nn)) + source.astype(F32)
    return total.astype(BF16)


def pack(m):
    t = TILE
    m = m.astype(F32)
    row, col = place_of((t, 2 * t))
    top, mid = m[:t, : 2 * t], m[t : 2 * t, : 2 * t]
    right = [widened(m[k * t : (k + 1) * t, 2 * t :]) for k in range(3)]
    left = col < t
    d1 = jnp.where(col == row + t, mid, 0.0)
    diagonal = jnp.sum(d1, axis=1, keepdims=True)
    spare = jnp.where(col == 0, diagonal, jnp.where((row == 2) & (col == 1), diagonal[:1], 0.0))
    shared = jnp.where(col - t >= row, half_turn(top), mid)
    last = jnp.where(col >= row, right[2], spare)
    return jnp.where(left, right[0], top), jnp.where(left, right[1], shared), last


def unpack(first, second, y):
    t = TILE
    row, col = place_of((t, 2 * t))
    left = col < t
    first_t, second_t = first.T, second.T
    t02, t01, t12, x_t = first_t[:t], first_t[t:], second_t[:t], second_t[t:]
    diagonal = jnp.where(row[:, :1] == 0, y[2:3, 1:2], y[:, :1])
    d0 = jnp.where(col >= row, half_turn(second), widened(x_t))
    d1 = jnp.where(
        col - t < row, second, jnp.where(col - t > row, widened(x_t), diagonal)
    )
    d2 = jnp.where((col >= row)[:, :t], y[:, :t], y[:, :t].T)
    wide = [
        jnp.where(left, d0, first),
        jnp.where(left, widened(t01), d1),
        jnp.where(left, widened(t02), widened(t12)),
    ]
    narrow = [first[:, :t], second[:, :t], d2]
    return jnp.concatenate(
        [jnp.concatenate(wide, axis=0), jnp.concatenate(narrow, axis=0)], axis=1
    ).astype(BF16)


def pack_pair(pair):
    (a_re, b_re, c_re), (a_im, b_im, c_im) = pack(pair[0]), pack(pair[1])
    _, col = place_of(c_re.shape)
    last = jnp.where(col < TILE, c_re, half_turn(c_im))
    return jnp.concatenate([a_re, b_re, a_im, b_im, last], axis=1)


def unpack_pair(p):
    p = p.astype(F32)
    parts = [p[:, 2 * TILE * k : 2 * TILE * (k + 1)] for k in range(5)]
    return unpack(parts[0], parts[1], parts[4]), unpack(parts[2], parts[3], half_turn(parts[4]))


def store_slabs(ref, start, packed):
    for k in range(5):
        ref[start + k * TILE : start + (k + 1) * TILE] = packed[:, 2 * k * TILE : 2 * (k + 1) * TILE]


def load_slabs(ref, start):
    slabs = [ref[start + k * TILE : start + (k + 1) * TILE] for k in range(5)]
    return jnp.concatenate(slabs, axis=1)


def store_map(ref, a, packed):
    n, w = 3 * TILE, 2 * TILE
    ref[:n] = a[0][:, :w]
    ref[n : 2 * n] = a[1][:, :w]
    ref[2 * n : 3 * n] = jnp.concatenate([a[0][:, w:], a[1][:, w:]], axis=1)
    store_slabs(ref, 3 * n, packed)


def load_map(ref):
    n, w = 3 * TILE, 2 * TILE
    rest = ref[2 * n : 3 * n]
    a = (
        jnp.concatenate([ref[:n], rest[:, :TILE]], axis=1),
        jnp.concatenate([ref[n : 2 * n], rest[:, TILE:]], axis=1),
    )
    return a, load_slabs(ref, 3 * n)


def load(ref, *at):
    return ref[(*at, 0)], ref[(*at, 1)]


def store(ref, pair, *at):
    ref[(*at, 0)] = pair[0]
    ref[(*at, 1)] = pair[1]


def local_kernel(
    green, coupling, screened, transfer, aggregate, green_in, coupling_in, screened_in, arrived
):
    copies = [
        [
            pltpu.make_async_copy(coupling.at[b], coupling_in.at[b], arrived.at[b, 0]),
            pltpu.make_async_copy(green.at[b, 0], green_in.at[b, 0], arrived.at[b, 1]),
            pltpu.make_async_copy(green.at[b, 1], green_in.at[b, 1], arrived.at[b, 2]),
        ]
        for b in range(2)
    ]
    later = [
        pltpu.make_async_copy(screened.at[b], screened_in.at[b], arrived.at[b, 3])
        for b in range(2)
    ]
    for copy in copies[0] + copies[1] + later:
        copy.start()
    maps = []
    for b in range(2):
        for copy in copies[b]:
            copy.wait()
        k = coupling_in[b]
        g = load(green_in, b)
        t = rounded((dot_nn(g[0], k), dot_nn(g[1], k)))
        if b == 0:
            store(transfer, t)
        maps.append((t, g))
    (t0, g0), (t1, g1) = maps
    c = pack_pair(sandwich(g0, t1, g1)).astype(BF16)
    store_map(aggregate, rounded(complex_product(t1, t0, dot_nn)), c)
    for b in range(2):
        later[b].wait()
        store_slabs(aggregate, MAP + b * PACKED, pack_pair(load(screened_in, b)).astype(BF16))


def joined(low, high):
    (a_low, c_low), (a_high, c_high) = load_map(low), load_map(high)
    a = rounded(complex_product(a_high, a_low, dot_nn))
    return a, sandwich_packed(unpack_pair(c_low), a_high, c_high)


def compose_kernel(maps, out):
    store_map(out, *joined(maps.at[0], maps.at[1]))


def middle_kernel(pairs, chips, end, before, onward):
    index = lax.axis_index("space")
    pair, odd = index // 4, index // 2 % 2 == 1
    first = load_slabs(pairs.at[0], 9 * TILE)
    before[...] = jnp.where(pair == 1, first, jnp.zeros_like(first))

    @pl.when(pair < 2)
    def _():
        end[...] = sandwich_packed(unpack_pair(first), *load_map(pairs.at[1]))

    @pl.when(pair >= 2)
    def _():
        end[...] = first

    @pl.when(pair < 3)
    def _():
        onward[...] = chips[0]

    @pl.when((pair == 3) & jnp.logical_not(odd))
    def _():
        onward[...] = pairs[0]

    @pl.when((pair == 3) & odd)
    def _():
        store_map(onward, *joined(pairs.at[0], chips.at[0]))


def rows_first(parts):
    return jnp.swapaxes(jnp.stack([p.astype(BF16) for p in parts], axis=0), 0, 1)


def entry_kernel(received, before_in, onward, entry, unused):
    index = lax.axis_index("space")
    pair, odd = index // 4, index // 2 % 2 == 1
    before = jnp.where(pair < 2, before_in[...], received[0])
    unused[...] = jnp.zeros(unused.shape, BF16)
    entry[TILE:] = jnp.zeros((TILE, 2 * PACKED), BF16)
    moved = odd | (pair == 3)

    @pl.when(moved)
    def _():
        entry[:TILE] = sandwich_packed(unpack_pair(before), *load_map(onward))

    @pl.when(jnp.logical_not(moved))
    def _():
        entry[:TILE] = before


def screen_kernel(cores, sent, last_map):
    last_map[...] = cores[0, :MAP]
    sent[...] = rows_first(
        [load_slabs(cores.at[core], MAP + b * PACKED) for core in range(2) for b in range(2)]
    )


def regroup_kernel(values, theirs, mine):
    x = jnp.swapaxes(values[...], 0, 1)
    points = values.shape[0]
    for b in range(2):
        mine[b] = x[b]
        theirs[b * points : (b + 1) * points] = x[2 + b]


def final_kernel(shared, cores, last_map, transfer, green, sent):
    odd = lax.axis_index("space") % 2 == 1

    def finish(entry, before):
        first = sandwich(before, load(transfer), load(green, 0))
        last = sandwich_packed(entry, *load_map(last_map))
        sent[...] = rows_first([pack_pair(first), last])

    @pl.when(odd)
    def _():
        entry = unpack_pair(shared[1, :TILE])
        a, c = load_map(cores.at[0])
        finish(entry, sandwich(entry, a, unpack_pair(c)))

    @pl.when(jnp.logical_not(odd))
    def _():
        entry = unpack_pair(shared[1, :TILE])
        finish(entry, entry)


def split(table):
    high = table.astype(jnp.bfloat16)
    return high, (table - high.astype(np.float32)).astype(jnp.bfloat16)


def tables(points):
    row = np.arange(points)
    angles = (row[:, None] * row[None, :] % points) * (2.0 * math.pi / points)
    cos, sin = np.cos(angles), np.sin(angles)
    forward = np.block([[cos, sin], [-sin, cos]]).astype(np.float32)
    scaling = 1.0 / (points * math.sqrt(points))
    inverse = (np.block([[-sin, -cos], [cos, -sin]]) * scaling).astype(np.float32)
    return np.concatenate(split(forward), axis=1), np.concatenate(split(inverse), axis=1)


def convolve_kernel(forward, inverse, values, shared, mine, out, screen):
    points, _, lanes = values.shape
    part = 4 * TILE
    even = lax.axis_index("space") % 2 == 0

    @pl.when(even)
    def _():
        screen[...] = mine[...]

    @pl.when(jnp.logical_not(even))
    def _():
        for b in range(2):
            screen[b] = shared[0, b * points : (b + 1) * points]

    g = jnp.swapaxes(values[...], 0, 1).astype(F32)
    x = [g[0], g[1], screen[0].astype(F32), screen[1].astype(F32)]
    _, col = place_of((points, 2 * TILE))
    left = col < TILE

    def mixed(first, second):
        return jnp.where(left, first, half_turn(second)), jnp.where(left, half_turn(first), second)

    re, im = [], []
    for k in (0, 2):
        last_re, last_im = mixed(x[k][:, 2 * part :], x[k + 1][:, 2 * part :])
        re += [x[k][:, :part], x[k + 1][:, :part], last_re]
        im += [x[k][:, part : 2 * part], x[k + 1][:, part : 2 * part], last_im]
    re = jnp.concatenate(re, axis=1).astype(BF16)
    im = jnp.concatenate(im, axis=1).astype(BF16)
    spectra = dot_nn(forward[...], jnp.concatenate([re, im, re, im], axis=0))
    g_re, g_im = spectra[:points, :lanes], spectra[points:, :lanes]
    s_re, s_im = spectra[:points, lanes:], spectra[points:, lanes:]
    product = jnp.concatenate([g_re * s_re - g_im * s_im, g_re * s_im + g_im * s_re], axis=0)
    high = product.astype(BF16)
    rest = (product - high.astype(F32)).astype(BF16)
    table = inverse[...]
    back = dot_nn(table, jnp.concatenate([high, high], axis=0)) + dot_nn(
        table[:, : 2 * points], rest
    )
    b_re, b_im = back[:points], back[points:]
    last = mixed(b_re[:, 2 * part :], b_im[:, 2 * part :])
    out[...] = rows_first(
        [
            jnp.concatenate(
                [b_re[:, b * part : (b + 1) * part], b_im[:, b * part : (b + 1) * part], last[b]],
                axis=1,
            )
            for b in range(2)
        ]
    )


def unpack_kernel(packed, out, block, left):
    parts = jnp.swapaxes(packed[...], 0, 1)
    copies = []
    for b in range(2):
        store(block, unpack_pair(parts[b]), b)
        copies.append(pltpu.make_async_copy(block.at[b], out.at[b], left.at[b]))
        copies[b].start()
    for copy in copies:
        copy.wait()


def call(kernel, out_shapes, specs, scratch=(), interpret=False, out_spec=VM):
    many = isinstance(out_shapes, (list, tuple))
    return pl.pallas_call(
        kernel,
        out_shape=out_shapes,
        in_specs=specs,
        out_specs=[out_spec] * len(out_shapes) if many else out_spec,
        scratch_shapes=scratch,
        compiler_params=pltpu.CompilerParams(vmem_limit_bytes=VMEM_GRANT),
        interpret=interpret,
    )


def shape(*dims):
    return jax.ShapeDtypeStruct(dims, BF16)


def chip_groups(pairs):
    return [[2 * low + core, 2 * high + core] for low, high in pairs for core in range(2)]


def scan_blocks(green, coupling, screened, exchange, interpret=False):
    n = green.shape[-1]
    transfer, aggregate = call(
        local_kernel,
        [shape(2, n, n), shape(MAP + 2 * PACKED, 2 * TILE)],
        [HB] * 3,
        scratch=[
            pltpu.VMEM((2, 2, n, n), BF16),
            pltpu.VMEM((2, n, n), BF16),
            pltpu.VMEM((2, 2, n, n), BF16),
            pltpu.SemaphoreType.DMA((2, 4)),
        ],
        interpret=interpret,
    )(*(pltpu.with_memory_space_constraint(x, pltpu.HBM) for x in (green, coupling, screened)))

    def gather(x, groups):
        return lax.all_gather(x, "space", axis_index_groups=groups)

    both = [[2 * c, 2 * c + 1] for c in range(8)]
    packed = shape(TILE, 2 * PACKED)
    points = TILE
    leaving = [shape(2 * points, 2 * PACKED), shape(2, points, 2 * PACKED)]

    def chain(cores):
        chip = call(compose_kernel, shape(MAP, 2 * TILE), [VM], interpret=interpret)(cores)
        chips = gather(chip, chip_groups([(0, 1), (2, 3), (4, 5), (6, 7)]))
        pair = call(compose_kernel, shape(MAP, 2 * TILE), [VM], interpret=interpret)(chips)
        pairs = gather(pair, chip_groups([(0, 2), (1, 3), (4, 6), (5, 7)]))
        end, before, onward = call(
            middle_kernel,
            [packed, packed, shape(MAP, 2 * TILE)],
            [VM] * 2,
            interpret=interpret,
        )(pairs, chips)
        received = gather(end, chip_groups([(0, 7), (1, 6), (2, 5), (3, 4)]))
        leave, unused = call(entry_kernel, leaving, [VM] * 3, interpret=interpret)(
            received, before, onward
        )
        return leave, unused, chip

    def exchange_screen(cores):
        sent, last_map = call(
            screen_kernel,
            [shape(TILE, 4, 2 * PACKED), shape(MAP, 2 * TILE)],
            [VM],
            interpret=interpret,
        )(cores)
        leave, mine = call(regroup_kernel, leaving, [VM], interpret=interpret)(exchange(sent))
        return leave, mine, last_map

    cores = gather(aggregate, both)
    odd = lax.axis_index("space") % 2 == 1
    leave, mine, last_map = lax.cond(odd, chain, exchange_screen, cores)
    shared = gather(leave, both)
    sent = call(
        final_kernel,
        shape(TILE, 2, 2 * PACKED),
        [VM] * 5,
        interpret=interpret,
    )(shared, cores, last_map, transfer, green)
    return sent, shared, mine


def shards(iso_green, coupling, screened):
    points = lax.axis_size("energy")
    n = iso_green.shape[-1]

    def exchange(x):
        return lax.all_to_all(x, "energy", split_axis=0, concat_axis=0, tiled=True)

    sent, shared, mine = scan_blocks(iso_green[0], coupling, screened[0], exchange)
    forward, inverse = tables(points)
    result = call(
        convolve_kernel,
        shape(points, 2, 2 * PACKED),
        [VM] * 5,
        scratch=[pltpu.VMEM((2, points, 2 * PACKED), BF16)],
    )(jnp.asarray(forward), jnp.asarray(inverse), exchange(sent), shared, mine)
    return call(
        unpack_kernel,
        shape(2, 2, n, n),
        [VM],
        scratch=[pltpu.VMEM((2, 2, n, n), BF16), pltpu.SemaphoreType.DMA((2,))],
        out_spec=HB,
    )(exchange(result))[None]


def solution(mesh):
    in_specs = (
        P("energy", "space", None, None, None),
        P("space", None, None),
        P("energy", "space", None, None, None),
    )
    out_specs = P("energy", "space", None, None, None)
    return jax.shard_map(shards, mesh=mesh, in_specs=in_specs, out_specs=out_specs, check_vma=False)
```

```python
import math

import jax
import jax.numpy as jnp
import numpy as np
from jax import lax
from jax.experimental import pallas as pl
from jax.experimental.pallas import tpu as pltpu
from jax.sharding import PartitionSpec as P

F32 = jnp.float32
BF16 = jnp.bfloat16
TILE = 64
PACKED = 5 * TILE
MAP = 14 * TILE
VMEM_GRANT = 16 * 2**20

VM = pl.BlockSpec(memory_space=pltpu.VMEM)
HB = pl.BlockSpec(memory_space=pltpu.HBM)


def dot_nn(a, b):
    return lax.dot_general(a, b, (((1,), (0,)), ((), ())), preferred_element_type=F32)


def dot_nt(a, b):
    return lax.dot_general(a, b, (((1,), (1,)), ((), ())), preferred_element_type=F32)


def complex_product(a, b, dot):
    a_re, a_im = a
    b_re, b_im = b
    return dot(a_re, b_re) - dot(a_im, b_im), dot(a_re, b_im) + dot(a_im, b_re)


def rounded(pair):
    return pair[0].astype(BF16), pair[1].astype(BF16)


def sandwich(carried, factor, source):
    middle = rounded(complex_product(carried, factor, dot_nt))
    re, im = complex_product(factor, middle, dot_nn)
    return rounded((source[0].astype(F32) + re, source[1].astype(F32) + im))


def half_turn(x):
    return pltpu.roll(x, TILE, 1)


def place_of(shape):
    row = lax.broadcasted_iota(jnp.int32, shape, 0)
    col = lax.broadcasted_iota(jnp.int32, shape, 1)
    return row, col


def widened(x):
    return jnp.concatenate([x, x], axis=1)


def sandwich_packed(carried, factor, source):
    middle = rounded(complex_product(carried, factor, dot_nt))
    total = pack_pair(complex_product(factor, middle, dot_nn)) + source.astype(F32)
    return total.astype(BF16)


def pack(m):
    t = TILE
    m = m.astype(F32)
    row, col = place_of((t, 2 * t))
    top, mid = m[:t, : 2 * t], m[t : 2 * t, : 2 * t]
    right = [widened(m[k * t : (k + 1) * t, 2 * t :]) for k in range(3)]
    left = col < t
    corner = (row == 2) & (col == 0)
    spare = jnp.where(corner, mid[:1, t : t + 1], jnp.where(col == row - 1, pltpu.roll(mid, t - 1, 1), 0.0))
    shared = jnp.where(col - t >= row, half_turn(top), mid)
    last = jnp.where(col >= row, right[2], spare)
    return jnp.where(left, right[0], top), jnp.where(left, right[1], shared), last


def unpack(first, second, y):
    t = TILE
    row, col = place_of((t, 2 * t))
    left = col < t
    first_t, second_t = first.T, second.T
    t02, t01, t12, x_t = first_t[:t], first_t[t:], second_t[:t], second_t[t:]
    diagonal = jnp.where(row == 0, y[2:3, :1], pltpu.roll(y, t + 1, 1))
    d0 = jnp.where(col >= row, half_turn(second), widened(x_t))
    d1 = jnp.where(
        col - t < row, second, jnp.where(col - t > row, widened(x_t), diagonal)
    )
    d2 = jnp.where((col >= row)[:, :t], y[:, :t], y[:, :t].T)
    wide = [
        jnp.where(left, d0, first),
        jnp.where(left, widened(t01), d1),
        jnp.where(left, widened(t02), widened(t12)),
    ]
    narrow = [first[:, :t], second[:, :t], d2]
    return jnp.concatenate(
        [jnp.concatenate(wide, axis=0), jnp.concatenate(narrow, axis=0)], axis=1
    ).astype(BF16)


def pack_pair(pair):
    (a_re, b_re, c_re), (a_im, b_im, c_im) = pack(pair[0]), pack(pair[1])
    _, col = place_of(c_re.shape)
    last = jnp.where(col < TILE, c_re, half_turn(c_im))
    return jnp.concatenate([a_re, b_re, a_im, b_im, last], axis=1)


def unpack_pair(p):
    p = p.astype(F32)
    parts = [p[:, 2 * TILE * k : 2 * TILE * (k + 1)] for k in range(5)]
    return unpack(parts[0], parts[1], parts[4]), unpack(parts[2], parts[3], half_turn(parts[4]))


def store_slabs(ref, start, packed):
    for k in range(5):
        ref[start + k * TILE : start + (k + 1) * TILE] = packed[:, 2 * k * TILE : 2 * (k + 1) * TILE]


def load_slabs(ref, start):
    slabs = [ref[start + k * TILE : start + (k + 1) * TILE] for k in range(5)]
    return jnp.concatenate(slabs, axis=1)


def store_map(ref, a, packed):
    n, w = 3 * TILE, 2 * TILE
    ref[:n] = a[0][:, :w]
    ref[n : 2 * n] = a[1][:, :w]
    ref[2 * n : 3 * n] = jnp.concatenate([a[0][:, w:], a[1][:, w:]], axis=1)
    store_slabs(ref, 3 * n, packed)


def load_map(ref):
    n, w = 3 * TILE, 2 * TILE
    rest = ref[2 * n : 3 * n]
    a = (
        jnp.concatenate([ref[:n], rest[:, :TILE]], axis=1),
        jnp.concatenate([ref[n : 2 * n], rest[:, TILE:]], axis=1),
    )
    return a, load_slabs(ref, 3 * n)


def load(ref, *at):
    return ref[(*at, 0)], ref[(*at, 1)]


def store(ref, pair, *at):
    ref[(*at, 0)] = pair[0]
    ref[(*at, 1)] = pair[1]


def local_kernel(
    green, coupling, screened, transfer, aggregate, green_in, coupling_in, screened_in, arrived
):
    copies = [
        [
            pltpu.make_async_copy(coupling.at[b], coupling_in.at[b], arrived.at[b, 0]),
            pltpu.make_async_copy(green.at[b, 0], green_in.at[b, 0], arrived.at[b, 1]),
            pltpu.make_async_copy(green.at[b, 1], green_in.at[b, 1], arrived.at[b, 2]),
        ]
        for b in range(2)
    ]
    later = [
        pltpu.make_async_copy(screened.at[b], screened_in.at[b], arrived.at[b, 3])
        for b in range(2)
    ]
    for copy in copies[0] + copies[1] + later:
        copy.start()
    maps = []
    for b in range(2):
        for copy in copies[b]:
            copy.wait()
        k = coupling_in[b]
        g = load(green_in, b)
        t = rounded((dot_nn(g[0], k), dot_nn(g[1], k)))
        if b == 0:
            store(transfer, t)
        maps.append((t, g))
    (t0, g0), (t1, g1) = maps
    c = pack_pair(sandwich(g0, t1, g1)).astype(BF16)
    store_map(aggregate, rounded(complex_product(t1, t0, dot_nn)), c)
    for b in range(2):
        later[b].wait()
        store_slabs(aggregate, MAP + b * PACKED, pack_pair(load(screened_in, b)).astype(BF16))


def joined(low, high):
    (a_low, c_low), (a_high, c_high) = load_map(low), load_map(high)
    a = rounded(complex_product(a_high, a_low, dot_nn))
    return a, sandwich_packed(unpack_pair(c_low), a_high, c_high)


def compose_kernel(maps, out):
    store_map(out, *joined(maps.at[0], maps.at[1]))


def middle_kernel(pairs, chips, end, before, onward):
    index = lax.axis_index("space")
    pair, odd = index // 4, index // 2 % 2 == 1
    first = load_slabs(pairs.at[0], 9 * TILE)
    before[...] = jnp.where(pair == 1, first, jnp.zeros_like(first))

    @pl.when(pair < 2)
    def _():
        end[...] = sandwich_packed(unpack_pair(first), *load_map(pairs.at[1]))

    @pl.when(pair >= 2)
    def _():
        end[...] = first

    @pl.when((pair == 3) & jnp.logical_not(odd))
    def _():
        onward[...] = pairs[0]

    @pl.when((pair == 3) & odd)
    def _():
        store_map(onward, *joined(pairs.at[0], chips.at[0]))


def rows_first(parts):
    return jnp.swapaxes(jnp.stack([p.astype(BF16) for p in parts], axis=0), 0, 1)


def entry_kernel(received, before_in, chips, onward, entry, unread):
    index = lax.axis_index("space")
    pair, odd = index // 4, index // 2 % 2 == 1
    before = jnp.where(pair < 2, before_in[...], received[0])

    @pl.when(pair == 3)
    def _():
        entry[:TILE] = sandwich_packed(unpack_pair(before), *load_map(onward))

    @pl.when((pair < 3) & odd)
    def _():
        entry[:TILE] = sandwich_packed(unpack_pair(before), *load_map(chips.at[0]))

    @pl.when((pair < 3) & jnp.logical_not(odd))
    def _():
        entry[:TILE] = before


def screen_kernel(cores, sent, last_map):
    last_map[...] = cores[0, :MAP]
    sent[...] = rows_first(
        [load_slabs(cores.at[core], MAP + b * PACKED) for core in range(2) for b in range(2)]
    )


def regroup_kernel(values, theirs, mine):
    x = jnp.swapaxes(values[...], 0, 1)
    points = values.shape[0]
    for b in range(2):
        mine[b] = x[b]
        theirs[b * points : (b + 1) * points] = x[2 + b]


def final_kernel(shared, cores, last_map, transfer, green, sent):
    odd = lax.axis_index("space") % 2 == 1

    def finish(entry, before):
        first = sandwich(before, load(transfer), load(green, 0))
        last = sandwich_packed(entry, *load_map(last_map))
        sent[...] = rows_first([pack_pair(first), last])

    @pl.when(odd)
    def _():
        entry = unpack_pair(shared[1, :TILE])
        a, c = load_map(cores.at[0])
        finish(entry, sandwich(entry, a, unpack_pair(c)))

    @pl.when(jnp.logical_not(odd))
    def _():
        entry = unpack_pair(shared[1, :TILE])
        finish(entry, entry)


def split(table):
    high = table.astype(jnp.bfloat16)
    return high, (table - high.astype(np.float32)).astype(jnp.bfloat16)


def tables(points):
    row = np.arange(points)
    angles = (row[:, None] * row[None, :] % points) * (2.0 * math.pi / points)
    cos, sin = np.cos(angles), np.sin(angles)
    forward = np.block([[cos, sin], [-sin, cos]]).astype(np.float32)
    scaling = 1.0 / (points * math.sqrt(points))
    inverse = (np.block([[-sin, -cos], [cos, -sin]]) * scaling).astype(np.float32)
    return np.concatenate(split(forward), axis=1), np.concatenate(split(inverse), axis=1)


def convolve_kernel(forward, inverse, values, shared, mine, out, screen):
    points, _, lanes = values.shape
    part = 4 * TILE
    even = lax.axis_index("space") % 2 == 0

    @pl.when(even)
    def _():
        screen[...] = mine[...]

    @pl.when(jnp.logical_not(even))
    def _():
        for b in range(2):
            screen[b] = shared[0, b * points : (b + 1) * points]

    g = jnp.swapaxes(values[...], 0, 1).astype(F32)
    x = [g[0], g[1], screen[0].astype(F32), screen[1].astype(F32)]
    _, col = place_of((points, 2 * TILE))
    left = col < TILE

    def mixed(first, second):
        return jnp.where(left, first, half_turn(second)), jnp.where(left, half_turn(first), second)

    re, im = [], []
    for k in (0, 2):
        last_re, last_im = mixed(x[k][:, 2 * part :], x[k + 1][:, 2 * part :])
        re += [x[k][:, :part], x[k + 1][:, :part], last_re]
        im += [x[k][:, part : 2 * part], x[k + 1][:, part : 2 * part], last_im]
    re = jnp.concatenate(re, axis=1).astype(BF16)
    im = jnp.concatenate(im, axis=1).astype(BF16)
    spectra = dot_nn(forward[...], jnp.concatenate([re, im, re, im], axis=0))
    g_re, g_im = spectra[:points, :lanes], spectra[points:, :lanes]
    s_re, s_im = spectra[:points, lanes:], spectra[points:, lanes:]
    product = jnp.concatenate([g_re * s_re - g_im * s_im, g_re * s_im + g_im * s_re], axis=0)
    high = product.astype(BF16)
    rest = (product - high.astype(F32)).astype(BF16)
    table = inverse[...]
    back = dot_nn(table, jnp.concatenate([high, high], axis=0)) + dot_nn(
        table[:, : 2 * points], rest
    )
    b_re, b_im = back[:points], back[points:]
    last = mixed(b_re[:, 2 * part :], b_im[:, 2 * part :])
    out[...] = rows_first(
        [
            jnp.concatenate(
                [b_re[:, b * part : (b + 1) * part], b_im[:, b * part : (b + 1) * part], last[b]],
                axis=1,
            )
            for b in range(2)
        ]
    )


def unpack_kernel(packed, out, block, left):
    parts = jnp.swapaxes(packed[...], 0, 1)
    copies = []
    for b in range(2):
        for part, matrix in enumerate(unpack_pair(parts[b])):
            block[b, part] = matrix
            copy = pltpu.make_async_copy(block.at[b, part], out.at[b, part], left.at[b, part])
            copy.start()
            copies.append(copy)
    for copy in copies:
        copy.wait()


def call(kernel, out_shapes, specs, scratch=(), interpret=False, out_spec=VM):
    many = isinstance(out_shapes, (list, tuple))
    return pl.pallas_call(
        kernel,
        out_shape=out_shapes,
        in_specs=specs,
        out_specs=[out_spec] * len(out_shapes) if many else out_spec,
        scratch_shapes=scratch,
        compiler_params=pltpu.CompilerParams(vmem_limit_bytes=VMEM_GRANT),
        interpret=interpret,
    )


def shape(*dims):
    return jax.ShapeDtypeStruct(dims, BF16)


def chip_groups(pairs):
    return [[2 * low + core, 2 * high + core] for low, high in pairs for core in range(2)]


def scan_blocks(green, coupling, screened, exchange, interpret=False):
    n = green.shape[-1]
    transfer, aggregate = call(
        local_kernel,
        [shape(2, n, n), shape(MAP + 2 * PACKED, 2 * TILE)],
        [HB] * 3,
        scratch=[
            pltpu.VMEM((2, 2, n, n), BF16),
            pltpu.VMEM((2, n, n), BF16),
            pltpu.VMEM((2, 2, n, n), BF16),
            pltpu.SemaphoreType.DMA((2, 4)),
        ],
        interpret=interpret,
    )(*(pltpu.with_memory_space_constraint(x, pltpu.HBM) for x in (green, coupling, screened)))

    def gather(x, groups):
        return lax.all_gather(x, "space", axis_index_groups=groups)

    both = [[2 * c, 2 * c + 1] for c in range(8)]
    packed = shape(TILE, 2 * PACKED)
    points = TILE
    leaving = [shape(2 * points, 2 * PACKED), shape(2, points, 2 * PACKED)]

    def chain(cores):
        chip = call(compose_kernel, shape(MAP, 2 * TILE), [VM], interpret=interpret)(cores)
        chips = gather(chip, chip_groups([(0, 1), (2, 3), (4, 5), (6, 7)]))
        pair = call(compose_kernel, shape(MAP, 2 * TILE), [VM], interpret=interpret)(chips)
        pairs = gather(pair, chip_groups([(0, 2), (1, 3), (4, 6), (5, 7)]))
        end, before, onward = call(
            middle_kernel,
            [packed, packed, shape(MAP, 2 * TILE)],
            [VM] * 2,
            interpret=interpret,
        )(pairs, chips)
        received = gather(end, chip_groups([(0, 7), (1, 6), (2, 5), (3, 4)]))
        leave, unused = call(entry_kernel, leaving, [VM] * 4, interpret=interpret)(
            received, before, chips, onward
        )
        return leave, unused, chip

    def exchange_screen(cores):
        sent, last_map = call(
            screen_kernel,
            [shape(TILE, 4, 2 * PACKED), shape(MAP, 2 * TILE)],
            [VM],
            interpret=interpret,
        )(cores)
        leave, mine = call(regroup_kernel, leaving, [VM], interpret=interpret)(exchange(sent))
        return leave, mine, last_map

    cores = gather(aggregate, both)
    odd = lax.axis_index("space") % 2 == 1
    leave, mine, last_map = lax.cond(odd, chain, exchange_screen, cores)
    shared = gather(leave, both)
    sent = call(
        final_kernel,
        shape(TILE, 2, 2 * PACKED),
        [VM] * 5,
        interpret=interpret,
    )(shared, cores, last_map, transfer, green)
    return sent, shared, mine


def shards(iso_green, coupling, screened):
    points = lax.axis_size("energy")
    n = iso_green.shape[-1]

    def exchange(x):
        return lax.all_to_all(x, "energy", split_axis=0, concat_axis=0, tiled=True)

    sent, shared, mine = scan_blocks(iso_green[0], coupling, screened[0], exchange)
    forward, inverse = tables(points)
    result = call(
        convolve_kernel,
        shape(points, 2, 2 * PACKED),
        [VM] * 5,
        scratch=[pltpu.VMEM((2, points, 2 * PACKED), BF16)],
    )(jnp.asarray(forward), jnp.asarray(inverse), exchange(sent), shared, mine)
    return call(
        unpack_kernel,
        shape(2, 2, n, n),
        [VM],
        scratch=[pltpu.VMEM((2, 2, n, n), BF16), pltpu.SemaphoreType.DMA((2, 2))],
        out_spec=HB,
    )(exchange(result))[None]


def solution(mesh):
    in_specs = (
        P("energy", "space", None, None, None),
        P("space", None, None),
        P("energy", "space", None, None, None),
    )
    out_specs = P("energy", "space", None, None, None)
    return jax.shard_map(shards, mesh=mesh, in_specs=in_specs, out_specs=out_specs, check_vma=False)
```

```python
import math

import jax
import jax.numpy as jnp
import numpy as np
from jax import lax
from jax.experimental import pallas as pl
from jax.experimental.pallas import tpu as pltpu
from jax.sharding import PartitionSpec as P

F32 = jnp.float32
BF16 = jnp.bfloat16
TILE = 64
PACKED = 5 * TILE
MAP = 14 * TILE
VMEM_GRANT = 16 * 2**20

VM = pl.BlockSpec(memory_space=pltpu.VMEM)
HB = pl.BlockSpec(memory_space=pltpu.HBM)


def dot_nn(a, b):
    return lax.dot_general(a, b, (((1,), (0,)), ((), ())), preferred_element_type=F32)


def dot_nt(a, b):
    return lax.dot_general(a, b, (((1,), (1,)), ((), ())), preferred_element_type=F32)


def complex_product(a, b, dot):
    a_re, a_im = a
    b_re, b_im = b
    return dot(a_re, b_re) - dot(a_im, b_im), dot(a_re, b_im) + dot(a_im, b_re)


def rounded(pair):
    return pair[0].astype(BF16), pair[1].astype(BF16)


def sandwich(carried, factor, source):
    middle = rounded(complex_product(carried, factor, dot_nt))
    re, im = complex_product(factor, middle, dot_nn)
    return rounded((source[0].astype(F32) + re, source[1].astype(F32) + im))


def half_turn(x):
    return pltpu.roll(x, TILE, 1)


def place_of(shape):
    row = lax.broadcasted_iota(jnp.int32, shape, 0)
    col = lax.broadcasted_iota(jnp.int32, shape, 1)
    return row, col


def widened(x):
    return jnp.concatenate([x, x], axis=1)


def sandwich_packed(carried, factor, source):
    middle = rounded(complex_product(carried, factor, dot_nt))
    total = pack_pair(complex_product(factor, middle, dot_nn)) + source.astype(F32)
    return total.astype(BF16)


def pack(m):
    t = TILE
    m = m.astype(F32)
    row, col = place_of((t, 2 * t))
    top, mid = m[:t, : 2 * t], m[t : 2 * t, : 2 * t]
    right = [widened(m[k * t : (k + 1) * t, 2 * t :]) for k in range(3)]
    left = col < t
    corner = (row == 2) & (col == 0)
    spare = jnp.where(corner, mid[:1, t : t + 1], jnp.where(col == row - 1, pltpu.roll(mid, t - 1, 1), 0.0))
    shared = jnp.where(col - t >= row, half_turn(top), mid)
    last = jnp.where(col >= row, right[2], spare)
    return jnp.where(left, right[0], top), jnp.where(left, right[1], shared), last


def unpack(first, second, y):
    t = TILE
    row, col = place_of((t, 2 * t))
    left = col < t
    first_t, second_t = first.T, second.T
    t02, t01, t12, x_t = first_t[:t], first_t[t:], second_t[:t], second_t[t:]
    diagonal = jnp.where(row == 0, y[2:3, :1], pltpu.roll(y, t + 1, 1))
    d0 = jnp.where(col >= row, half_turn(second), widened(x_t))
    d1 = jnp.where(
        col - t < row, second, jnp.where(col - t > row, widened(x_t), diagonal)
    )
    d2 = jnp.where((col >= row)[:, :t], y[:, :t], y[:, :t].T)
    wide = [
        jnp.where(left, d0, first),
        jnp.where(left, widened(t01), d1),
        jnp.where(left, widened(t02), widened(t12)),
    ]
    narrow = [first[:, :t], second[:, :t], d2]
    return jnp.concatenate(
        [jnp.concatenate(wide, axis=0), jnp.concatenate(narrow, axis=0)], axis=1
    ).astype(BF16)


def pack_pair(pair):
    (a_re, b_re, c_re), (a_im, b_im, c_im) = pack(pair[0]), pack(pair[1])
    _, col = place_of(c_re.shape)
    last = jnp.where(col < TILE, c_re, half_turn(c_im))
    return jnp.concatenate([a_re, b_re, a_im, b_im, last], axis=1)


def unpack_pair(p):
    p = p.astype(F32)
    parts = [p[:, 2 * TILE * k : 2 * TILE * (k + 1)] for k in range(5)]
    return unpack(parts[0], parts[1], parts[4]), unpack(parts[2], parts[3], half_turn(parts[4]))


def store_slabs(ref, start, packed):
    for k in range(5):
        ref[start + k * TILE : start + (k + 1) * TILE] = packed[:, 2 * k * TILE : 2 * (k + 1) * TILE]


def load_slabs(ref, start):
    slabs = [ref[start + k * TILE : start + (k + 1) * TILE] for k in range(5)]
    return jnp.concatenate(slabs, axis=1)


def store_map(ref, a, packed):
    n, w = 3 * TILE, 2 * TILE
    ref[:n] = a[0][:, :w]
    ref[n : 2 * n] = a[1][:, :w]
    ref[2 * n : 3 * n] = jnp.concatenate([a[0][:, w:], a[1][:, w:]], axis=1)
    store_slabs(ref, 3 * n, packed)


def load_map(ref):
    n, w = 3 * TILE, 2 * TILE
    rest = ref[2 * n : 3 * n]
    a = (
        jnp.concatenate([ref[:n], rest[:, :TILE]], axis=1),
        jnp.concatenate([ref[n : 2 * n], rest[:, TILE:]], axis=1),
    )
    return a, load_slabs(ref, 3 * n)


def load(ref, *at):
    return ref[(*at, 0)], ref[(*at, 1)]


def store(ref, pair, *at):
    ref[(*at, 0)] = pair[0]
    ref[(*at, 1)] = pair[1]


def local_kernel(
    green, coupling, screened, transfer, own, sent, green_in, coupling_in, screened_in, arrived
):
    odd = lax.axis_index("space") % 2 == 1
    copies = [
        [
            pltpu.make_async_copy(coupling.at[b], coupling_in.at[b], arrived.at[b, 0]),
            pltpu.make_async_copy(green.at[b, 0], green_in.at[b, 0], arrived.at[b, 1]),
            pltpu.make_async_copy(green.at[b, 1], green_in.at[b, 1], arrived.at[b, 2]),
        ]
        for b in range(2)
    ]
    later = [
        pltpu.make_async_copy(screened.at[b], screened_in.at[b], arrived.at[b, 3])
        for b in range(2)
    ]
    for copy in copies[0] + copies[1]:
        copy.start()

    @pl.when(odd)
    def _():
        for copy in later:
            copy.start()

    maps = []
    for b in range(2):
        for copy in copies[b]:
            copy.wait()
        k = coupling_in[b]
        g = load(green_in, b)
        t = rounded((dot_nn(g[0], k), dot_nn(g[1], k)))
        if b == 0:
            store(transfer, t)
        maps.append((t, g))
    (t0, g0), (t1, g1) = maps
    c = pack_pair(sandwich(g0, t1, g1)).astype(BF16)
    store_map(own, rounded(complex_product(t1, t0, dot_nn)), c)

    @pl.when(odd)
    def _():
        for b in range(2):
            later[b].wait()
            store_slabs(sent, b * PACKED, pack_pair(load(screened_in, b)).astype(BF16))

    @pl.when(jnp.logical_not(odd))
    def _():
        sent[...] = own[...]


def joined(low, high):
    (a_low, c_low), (a_high, c_high) = load_map(low), load_map(high)
    a = rounded(complex_product(a_high, a_low, dot_nn))
    return a, sandwich_packed(unpack_pair(c_low), a_high, c_high)


def compose_kernel(maps, out):
    store_map(out, *joined(maps.at[0], maps.at[1]))


def chip_kernel(cores, own, out):
    store_map(out, *joined(cores.at[0], own))


def middle_kernel(pairs, chips, end, before, onward):
    index = lax.axis_index("space")
    pair, odd = index // 4, index // 2 % 2 == 1
    first = load_slabs(pairs.at[0], 9 * TILE)
    before[...] = jnp.where(pair == 1, first, jnp.zeros_like(first))

    @pl.when(pair < 2)
    def _():
        end[...] = sandwich_packed(unpack_pair(first), *load_map(pairs.at[1]))

    @pl.when(pair >= 2)
    def _():
        end[...] = first

    @pl.when((pair == 3) & jnp.logical_not(odd))
    def _():
        onward[...] = pairs[0]

    @pl.when((pair == 3) & odd)
    def _():
        store_map(onward, *joined(pairs.at[0], chips.at[0]))


def rows_first(parts):
    return jnp.swapaxes(jnp.stack([p.astype(BF16) for p in parts], axis=0), 0, 1)


def entry_kernel(received, before_in, chips, onward, entry, unread):
    index = lax.axis_index("space")
    pair, odd = index // 4, index // 2 % 2 == 1
    before = jnp.where(pair < 2, before_in[...], received[0])

    @pl.when(pair == 3)
    def _():
        entry[:TILE] = sandwich_packed(unpack_pair(before), *load_map(onward))

    @pl.when((pair < 3) & odd)
    def _():
        entry[:TILE] = sandwich_packed(unpack_pair(before), *load_map(chips.at[0]))

    @pl.when((pair < 3) & jnp.logical_not(odd))
    def _():
        entry[:TILE] = before


def screen_kernel(cores, own, screened, sent, last_map):
    last_map[...] = own[...]
    mine = [pack_pair(load(screened, b)).astype(BF16) for b in range(2)]
    sent[...] = rows_first(mine + [load_slabs(cores.at[1], b * PACKED) for b in range(2)])


def regroup_kernel(values, theirs, mine):
    x = jnp.swapaxes(values[...], 0, 1)
    points = values.shape[0]
    for b in range(2):
        mine[b] = x[b]
        theirs[b * points : (b + 1) * points] = x[2 + b]


def final_kernel(shared, cores, last_map, transfer, green, sent):
    odd = lax.axis_index("space") % 2 == 1

    def finish(entry, before):
        first = sandwich(before, load(transfer), load(green, 0))
        last = sandwich_packed(entry, *load_map(last_map))
        sent[...] = rows_first([pack_pair(first), last])

    @pl.when(odd)
    def _():
        entry = unpack_pair(shared[1, :TILE])
        a, c = load_map(cores.at[0])
        finish(entry, sandwich(entry, a, unpack_pair(c)))

    @pl.when(jnp.logical_not(odd))
    def _():
        entry = unpack_pair(shared[1, :TILE])
        finish(entry, entry)


def split(table):
    high = table.astype(jnp.bfloat16)
    return high, (table - high.astype(np.float32)).astype(jnp.bfloat16)


def tables(points):
    row = np.arange(points)
    angles = (row[:, None] * row[None, :] % points) * (2.0 * math.pi / points)
    cos, sin = np.cos(angles), np.sin(angles)
    forward = np.block([[cos, sin], [-sin, cos]]).astype(np.float32)
    scaling = 1.0 / (points * math.sqrt(points))
    inverse = (np.block([[-sin, -cos], [cos, -sin]]) * scaling).astype(np.float32)
    return np.concatenate(split(forward), axis=1), np.concatenate(split(inverse), axis=1)


def convolve_kernel(forward, inverse, values, shared, mine, out, screen):
    points, _, lanes = values.shape
    part = 4 * TILE
    even = lax.axis_index("space") % 2 == 0

    @pl.when(even)
    def _():
        screen[...] = mine[...]

    @pl.when(jnp.logical_not(even))
    def _():
        for b in range(2):
            screen[b] = shared[0, b * points : (b + 1) * points]

    g = jnp.swapaxes(values[...], 0, 1).astype(F32)
    x = [g[0], g[1], screen[0].astype(F32), screen[1].astype(F32)]
    _, col = place_of((points, 2 * TILE))
    left = col < TILE

    def mixed(first, second):
        return jnp.where(left, first, half_turn(second)), jnp.where(left, half_turn(first), second)

    re, im = [], []
    for k in (0, 2):
        last_re, last_im = mixed(x[k][:, 2 * part :], x[k + 1][:, 2 * part :])
        re += [x[k][:, :part], x[k + 1][:, :part], last_re]
        im += [x[k][:, part : 2 * part], x[k + 1][:, part : 2 * part], last_im]
    re = jnp.concatenate(re, axis=1).astype(BF16)
    im = jnp.concatenate(im, axis=1).astype(BF16)
    spectra = dot_nn(forward[...], jnp.concatenate([re, im, re, im], axis=0))
    g_re, g_im = spectra[:points, :lanes], spectra[points:, :lanes]
    s_re, s_im = spectra[:points, lanes:], spectra[points:, lanes:]
    product = jnp.concatenate([g_re * s_re - g_im * s_im, g_re * s_im + g_im * s_re], axis=0)
    high = product.astype(BF16)
    rest = (product - high.astype(F32)).astype(BF16)
    table = inverse[...]
    back = dot_nn(table, jnp.concatenate([high, high], axis=0)) + dot_nn(
        table[:, : 2 * points], rest
    )
    b_re, b_im = back[:points], back[points:]
    last = mixed(b_re[:, 2 * part :], b_im[:, 2 * part :])
    out[...] = rows_first(
        [
            jnp.concatenate(
                [b_re[:, b * part : (b + 1) * part], b_im[:, b * part : (b + 1) * part], last[b]],
                axis=1,
            )
            for b in range(2)
        ]
    )


def unpack_kernel(packed, out, block, left):
    parts = jnp.swapaxes(packed[...], 0, 1)
    copies = []
    for b in range(2):
        for part, matrix in enumerate(unpack_pair(parts[b])):
            block[b, part] = matrix
            copy = pltpu.make_async_copy(block.at[b, part], out.at[b, part], left.at[b, part])
            copy.start()
            copies.append(copy)
    for copy in copies:
        copy.wait()


def call(kernel, out_shapes, specs, scratch=(), interpret=False, out_spec=VM):
    many = isinstance(out_shapes, (list, tuple))
    return pl.pallas_call(
        kernel,
        out_shape=out_shapes,
        in_specs=specs,
        out_specs=[out_spec] * len(out_shapes) if many else out_spec,
        scratch_shapes=scratch,
        compiler_params=pltpu.CompilerParams(vmem_limit_bytes=VMEM_GRANT),
        interpret=interpret,
    )


def shape(*dims):
    return jax.ShapeDtypeStruct(dims, BF16)


def chip_groups(pairs):
    return [[2 * low + core, 2 * high + core] for low, high in pairs for core in range(2)]


def scan_blocks(green, coupling, screened, exchange, interpret=False):
    n = green.shape[-1]
    transfer, own, aggregate = call(
        local_kernel,
        [shape(2, n, n), shape(MAP, 2 * TILE), shape(MAP, 2 * TILE)],
        [HB] * 3,
        scratch=[
            pltpu.VMEM((2, 2, n, n), BF16),
            pltpu.VMEM((2, n, n), BF16),
            pltpu.VMEM((2, 2, n, n), BF16),
            pltpu.SemaphoreType.DMA((2, 4)),
        ],
        interpret=interpret,
    )(*(pltpu.with_memory_space_constraint(x, pltpu.HBM) for x in (green, coupling, screened)))

    def gather(x, groups):
        return lax.all_gather(x, "space", axis_index_groups=groups)

    both = [[2 * c, 2 * c + 1] for c in range(8)]
    packed = shape(TILE, 2 * PACKED)
    points = TILE
    leaving = [shape(2 * points, 2 * PACKED), shape(2, points, 2 * PACKED)]

    def chain(cores, own, screened):
        chip = call(chip_kernel, shape(MAP, 2 * TILE), [VM] * 2, interpret=interpret)(cores, own)
        chips = gather(chip, chip_groups([(0, 1), (2, 3), (4, 5), (6, 7)]))
        pair = call(compose_kernel, shape(MAP, 2 * TILE), [VM], interpret=interpret)(chips)
        pairs = gather(pair, chip_groups([(0, 2), (1, 3), (4, 6), (5, 7)]))
        end, before, onward = call(
            middle_kernel,
            [packed, packed, shape(MAP, 2 * TILE)],
            [VM] * 2,
            interpret=interpret,
        )(pairs, chips)
        received = gather(end, chip_groups([(0, 7), (1, 6), (2, 5), (3, 4)]))
        leave, unused = call(entry_kernel, leaving, [VM] * 4, interpret=interpret)(
            received, before, chips, onward
        )
        return leave, unused, chip

    def exchange_screen(cores, own, screened):
        sent, last_map = call(
            screen_kernel,
            [shape(TILE, 4, 2 * PACKED), shape(MAP, 2 * TILE)],
            [VM] * 3,
            interpret=interpret,
        )(cores, own, screened)
        leave, mine = call(regroup_kernel, leaving, [VM], interpret=interpret)(exchange(sent))
        return leave, mine, last_map

    cores = gather(aggregate, both)
    odd = lax.axis_index("space") % 2 == 1
    leave, mine, last_map = lax.cond(odd, chain, exchange_screen, cores, own, screened)
    shared = gather(leave, both)
    sent = call(
        final_kernel,
        shape(TILE, 2, 2 * PACKED),
        [VM] * 5,
        interpret=interpret,
    )(shared, cores, last_map, transfer, green)
    return sent, shared, mine


def shards(iso_green, coupling, screened):
    points = lax.axis_size("energy")
    n = iso_green.shape[-1]

    def exchange(x):
        return lax.all_to_all(x, "energy", split_axis=0, concat_axis=0, tiled=True)

    sent, shared, mine = scan_blocks(iso_green[0], coupling, screened[0], exchange)
    forward, inverse = tables(points)
    result = call(
        convolve_kernel,
        shape(points, 2, 2 * PACKED),
        [VM] * 5,
        scratch=[pltpu.VMEM((2, points, 2 * PACKED), BF16)],
    )(jnp.asarray(forward), jnp.asarray(inverse), exchange(sent), shared, mine)
    return call(
        unpack_kernel,
        shape(2, 2, n, n),
        [VM],
        scratch=[pltpu.VMEM((2, 2, n, n), BF16), pltpu.SemaphoreType.DMA((2, 2))],
        out_spec=HB,
    )(exchange(result))[None]


def solution(mesh):
    in_specs = (
        P("energy", "space", None, None, None),
        P("space", None, None),
        P("energy", "space", None, None, None),
    )
    out_specs = P("energy", "space", None, None, None)
    return jax.shard_map(shards, mesh=mesh, in_specs=in_specs, out_specs=out_specs, check_vma=False)
```
